512 devices in a mesh: ex: 16 (over z, x_hi), feat: 32 (over x_lo, y, core).
Axes of the slice: x: 4 (x_hi: 2, x_lo: 2; x = x_hi * 2 + x_lo), y: 8, z: 8, core: 2. Of those that a mesh axis runs over, the one named last changes fastest.
Arguments:
- features: bfloat16 [16384, 2048], P('ex', 'feat')
- centre_index: int32 [32, 16, 16], P(None, 'ex'), may hold values from 0 to 16383, as said below
- labels: int32 [16384], P('ex'), may hold values from 0 to 15
- precond: float32 [8192, 256], P('feat'), as said below
Outputs:
- predictions: float32 [16384, 16], P('ex')
The draws below stay inside these ranges and needn't reach their ends.
Inputs may be any that keep to these rules, and one draw needn't show every extreme that they name: centre_index[j, i, c] lies among the examples i * 1024 to (i + 1) * 1024 - 1, and all entries are different. Each 256 x 256 block of precond is symmetric, and its diagonal entry exceeds the sum of the magnitudes of the other entries of its row by at least half of itself.
All inputs are finite; a program needn't handle non-finite values.
Results may differ from the reference program's by a relative error of at most 0.0003.
Values may be sent and summed in bfloat16 or wider, within the bound.
No kernel may reach another device: no remote copies, remote signals or barrier semaphores. Data moves between devices by JAX's collectives and lax.ppermute only.
A program may use at most 64 MiB of HBM per device.

```python
import math
import jax
import jax.numpy as jnp
from jax import lax

F = 2048
CLASS_COUNT = 16
ROWS_DEV = 1024
CB = 16
ITERS = 2
EXAMPLES = 16384
CENTRES_PER_BLOCK = 256
CENTRES = 8192
N_EX = 16
N_FEAT = 32


def draw_features(key, part):
    random_keys = jax.random.split(key, 5)
    noise = jax.random.normal(random_keys[0], (EXAMPLES, F), jnp.float32)
    groups = jnp.clip(jax.random.normal(random_keys[1], (EXAMPLES, 16), jnp.float32), -3.0, 3.0)
    pattern = jnp.clip(jax.random.normal(random_keys[2], (F // 16, 16), jnp.float32), -3.0, 3.0)
    mixed = (noise.reshape(EXAMPLES, F // 16, 16) + groups[:, None, :] * pattern[None, :, :]).reshape(EXAMPLES, F)
    col_scale = jnp.exp(jax.random.uniform(random_keys[4], (1, F), jnp.float32, 0.0, math.log(3.0)))
    mixed = mixed * col_scale
    unit = mixed * lax_rsqrt_mean(mixed)
    row_scale = jnp.exp(jax.random.uniform(random_keys[3], (EXAMPLES, 1), jnp.float32, 0.0, math.log(10.0)))
    return (unit * row_scale).astype(jnp.bfloat16)


def lax_rsqrt_mean(mixed):
    return 1.0 / jnp.sqrt(jnp.mean(mixed * mixed, axis=1, keepdims=True) + 1e-06)


def draw_centre_index(key, part):

    def one_block(block):
        picked = jax.random.permutation(jax.random.fold_in(key, block), ROWS_DEV)[:N_FEAT * CB]
        return (picked.astype(jnp.int32) + block * ROWS_DEV).reshape(N_FEAT, CB)
    stacked = jax.vmap(one_block)(jnp.arange(N_EX, dtype=jnp.int32))
    return jnp.transpose(stacked, (1, 0, 2)).astype(jnp.int32)


def draw_precond(key, part):
    random_keys = jax.random.split(key, 2)
    off_diagonal_blocks = jax.random.uniform(random_keys[0], (N_FEAT, CENTRES_PER_BLOCK, CENTRES_PER_BLOCK), jnp.float32, -1.0, 1.0) * (0.3 / CENTRES_PER_BLOCK)
    sym = 0.5 * (off_diagonal_blocks + jnp.swapaxes(off_diagonal_blocks, 1, 2))
    diagonal_blocks = jnp.exp(jax.random.uniform(random_keys[1], (N_FEAT, CENTRES_PER_BLOCK), jnp.float32, 0.0, math.log(3.0)))
    identity_matrix = jnp.eye(CENTRES_PER_BLOCK, dtype=jnp.float32)
    block_matrices = sym * (1.0 - identity_matrix)[None] + identity_matrix[None] * diagonal_blocks[:, None, :]
    return block_matrices.reshape(N_FEAT * CENTRES_PER_BLOCK, CENTRES_PER_BLOCK)


def touch_ends(values, rng, low, high):
    longest = values.shape.index(max(values.shape))
    spots = []
    for shift in (0, 1):
        where = [jax.random.randint(jax.random.fold_in(rng, axis), (), 0, length) for axis, length in enumerate(values.shape)]
        where[longest] = (where[longest] + shift) % values.shape[longest]
        spots.append(tuple(where))
    return values.at[spots[0]].set(low).at[spots[1]].set(high)


def setup_inputs(seed: int = 0) -> dict:
    key_of = jax.random.split(jax.random.key(seed), 5)
    features = draw_features(jax.random.fold_in(key_of[4], 71), 0)
    centre_index = draw_centre_index(jax.random.fold_in(key_of[4], 71), 0)
    labels = touch_ends(jax.random.randint(key_of[2], (EXAMPLES,), 0, CLASS_COUNT), jax.random.fold_in(key_of[2], 1), 0, CLASS_COUNT - 1).astype(jnp.int32)
    precond = draw_precond(jax.random.fold_in(key_of[4], 71), 0)
    return {"features": features, "centre_index": centre_index, "labels": labels, "precond": precond}


GAMMA = 4.0
LAMBDA = 0.05
EPS = 1e-06
HIGH = lax.Precision.HIGHEST

def reference(features, centre_index, labels, precond):
    idx = centre_index.reshape(-1).astype(jnp.int32)
    scale = lax.rsqrt(lax.optimization_barrier(jnp.mean(jnp.square(features.astype(jnp.float32)), axis=1)) + EPS)
    centres = jnp.take(features, idx, axis=0)
    centre_scale = jnp.take(scale, idx, axis=0)
    row_block = min(ROWS_DEV, 1024)
    count = EXAMPLES // row_block
    blocks = features.reshape(count, row_block, F)
    block_scale = scale.reshape(count, row_block)

    def make_block(pair):
        rows, rows_scale = pair
        dots = jnp.dot(rows, centres.T, preferred_element_type=jnp.float32)
        cosine = jnp.clip(dots * rows_scale[:, None] * centre_scale[None, :], -1.0, 1.0)
        return jnp.exp(GAMMA * (cosine - 1.0))
    panel = lax.map(make_block, (blocks, block_scale)).reshape(EXAMPLES, CENTRES)
    onehot = (labels[:, None] == jnp.arange(CLASS_COUNT, dtype=jnp.int32)[None, :]).astype(jnp.float32)
    targets = CLASS_COUNT * onehot - 1.0
    rhs = jnp.dot(panel.T, targets, precision=HIGH) / EXAMPLES

    def apply_normal(vec):
        kvec = jnp.dot(panel, vec, precision=HIGH)
        return jnp.dot(panel.T, kvec, precision=HIGH) / EXAMPLES + LAMBDA * jnp.take(kvec, idx, axis=0)
    block_preconditioners = precond.reshape(N_FEAT, CENTRES_PER_BLOCK, CENTRES_PER_BLOCK)

    def apply_pre(residual_vector):
        partial_pieces = residual_vector.reshape(N_FEAT, CENTRES_PER_BLOCK, CLASS_COUNT)
        return jnp.einsum('bkl,blc->bkc', block_preconditioners, partial_pieces, precision=HIGH).reshape(CENTRES, CLASS_COUNT)
    weights = jnp.zeros((CENTRES, CLASS_COUNT), jnp.float32)
    residual = rhs
    precon_res = apply_pre(residual)
    direction = precon_res
    rz_now = lax.optimization_barrier(jnp.sum(residual * precon_res, axis=0))
    for step in range(ITERS):
        image = apply_normal(direction)
        alpha = rz_now / lax.optimization_barrier(jnp.sum(direction * image, axis=0))
        weights = weights + alpha * direction
        residual = residual - alpha * image
        precon_res = apply_pre(residual)
        rz_next = lax.optimization_barrier(jnp.sum(residual * precon_res, axis=0))
        direction = precon_res + rz_next / rz_now * direction
        rz_now = rz_next
    return jnp.dot(panel, weights, precision=HIGH)
```

```python
import functools

import jax
import jax.numpy as jnp
from jax import lax
from jax.experimental import pallas as pl
from jax.experimental.pallas import tpu as pltpu
from jax.sharding import Mesh, PartitionSpec as P

CLASSES = 16
GAMMA = 4.0
LAMBDA = 0.05
EPS = 1e-06
HIGH = lax.Precision.HIGHEST
F32 = jnp.float32
BF16 = jnp.bfloat16

ROWS = 1024
BLOCK = 256
OWN = 16
N_EX = 16
N_FEAT = 32
N_PLANE = 16
SLICE = 64
WIDTH = N_PLANE * SLICE
F = 2048
EXAMPLES = ROWS * N_EX

EX = ("z", "xh")
PLANE = ("xl", "y")
FEAT = ("xl", "y", "c")

LANES = (((1,), (1,)), ((), ()))


def dot_t(a, b, precision=HIGH):
    return lax.dot_general(a, b, LANES, precision=precision, preferred_element_type=F32)


def iota(shape, dim):
    return lax.broadcasted_iota(jnp.int32, shape, dim)


def to_row(col, offset=0):
    n = col.shape[0]
    place = iota((n, 128), 1) == iota((n, 128), 0) + offset
    return jnp.sum(jnp.where(place, col, 0.0), axis=0, keepdims=True)


def to_col(row, n, offset=0):
    place = iota((n, 128), 1) == iota((n, 128), 0) + offset
    return jnp.sum(jnp.where(place, row, 0.0), axis=1, keepdims=True)


def call(kernel, outs, *args, name, smem=0):
    spec = [pl.BlockSpec(memory_space=pltpu.SMEM)] * smem
    spec += [pl.BlockSpec(memory_space=pltpu.VMEM)] * (len(args) - smem)
    many = isinstance(outs, list)
    out_spec = pl.BlockSpec(memory_space=pltpu.VMEM)
    return pl.pallas_call(
        kernel,
        out_shape=[jax.ShapeDtypeStruct(s, d) for s, d in outs] if many else jax.ShapeDtypeStruct(*outs),
        in_specs=spec,
        out_specs=[out_spec] * len(outs) if many else out_spec,
        name=name,
    )(*args)


def pick_kernel(ft_ref, own_ref, other_ref, out_ref):
    ft = ft_ref[...]
    zero = jnp.zeros_like(ft)
    n = N_PLANE * OWN
    lane = iota((n, ROWS), 1)

    def chosen(index_ref, table):
        mask = (lane == index_ref[...]).astype(F32).astype(BF16)
        return lax.dot_general(mask, table, LANES, preferred_element_type=F32)

    both = chosen(own_ref, jnp.concatenate([ft, zero], axis=0))
    both = both + chosen(other_ref, jnp.concatenate([zero, ft], axis=0))
    out_ref[...] = both.astype(BF16).reshape(N_PLANE, OWN, 2 * SLICE)


def spread_kernel(in_ref, out_ref):
    low = iota((OWN, 128), 1) < SLICE
    for t in range(N_PLANE // 2):
        a = in_ref[2 * t].astype(F32)
        b = in_ref[2 * t + 1].astype(F32)
        own = jnp.where(low, a, pltpu.roll(b, SLICE, 1)).astype(BF16)
        other = jnp.where(low, pltpu.roll(a, SLICE, 1), b).astype(BF16)
        cols = slice(128 * t, 128 * t + 128)
        for i in range(N_EX):
            out_ref[i, 0:OWN, cols] = own
            out_ref[i, OWN : 2 * OWN, cols] = other


def half_dots(ft_ref, cen_ref, first):
    block = cen_ref[:, first : first + OWN, :].reshape(BLOCK, WIDTH)
    dots = jnp.dot(block, ft_ref[...], preferred_element_type=F32)
    squares = jnp.sum(jnp.square(block.astype(F32)), axis=1, keepdims=True)
    return dots, squares


def other_kernel(ft_ref, cen_ref, out_ref):
    dots, squares = half_dots(ft_ref, cen_ref, OWN)
    out_ref[0:BLOCK, :] = dots
    out_ref[BLOCK : BLOCK + 8, :] = jnp.zeros((8, ROWS), F32)
    out_ref[BLOCK : BLOCK + 1, :] = jnp.sum(jnp.square(ft_ref[...].astype(F32)), axis=0, keepdims=True)
    same = iota((BLOCK, BLOCK), 0) == iota((BLOCK, BLOCK), 1)
    out_ref[BLOCK + 1 : BLOCK + 2, 0:BLOCK] = jnp.sum(jnp.where(same, squares, 0.0), axis=0, keepdims=True)


def own_kernel(ft_ref, cen_ref, dots_ref, squares_ref):
    dots, squares = half_dots(ft_ref, cen_ref, 0)
    dots_ref[...] = dots
    squares_ref[...] = jnp.broadcast_to(squares, (BLOCK, 128))


def panel_kernel(dots_ref, squares_ref, sent_ref, recv_ref, labels_ref, loc_ref, panel_ref, normal_ref, out_ref):
    row_sq = sent_ref[BLOCK : BLOCK + 1, :] + recv_ref[BLOCK : BLOCK + 1, :]
    same = iota((BLOCK, BLOCK), 0) == iota((BLOCK, BLOCK), 1)
    got = jnp.sum(jnp.where(same, recv_ref[BLOCK + 1 : BLOCK + 2, 0:BLOCK], 0.0), axis=1, keepdims=True)
    row_scale = lax.rsqrt(row_sq / F + EPS)
    centre_scale = lax.rsqrt((squares_ref[:, 0:1] + got) / F + EPS)
    dots = dots_ref[...] + recv_ref[0:BLOCK, :]
    cosine = jnp.clip(dots * row_scale * centre_scale, -1.0, 1.0)
    panel = jnp.exp(GAMMA * (cosine - 1.0))
    panel_ref[...] = panel
    placed = iota((BLOCK, ROWS), 1) == loc_ref[...]
    normal_ref[...] = panel / EXAMPLES + jnp.where(placed, LAMBDA, 0.0)
    hit = iota((CLASSES, ROWS), 0) == labels_ref[...]
    targets = jnp.where(hit, CLASSES - 1.0, -1.0)
    rhs = dot_t(targets, panel) / EXAMPLES
    for i in range(N_EX):
        out_ref[i] = rhs


def total(ref):
    acc = ref[0]
    for i in range(1, ref.shape[0]):
        acc = acc + ref[i]
    return acc


def put_chunks(out_ref, vec, stride, slot):
    for s in range(N_FEAT):
        g, l = s // 8, s % 8
        out_ref[s * stride + slot] = vec[4 * g : 4 * g + 4, 128 * l : 128 * l + 128]


def take_chunks(in_ref, stride, out_ref):
    for s in range(N_FEAT):
        g, l = s // 8, s % 8
        out_ref[4 * g : 4 * g + 4, 128 * l : 128 * l + 128] = in_ref[s * stride]


def sum_slot(ref, stride, slot):
    acc = ref[slot]
    for s in range(1, N_FEAT):
        acc = acc + ref[s * stride + slot]
    return acc


def first_kernel(recv_ref, pre_ref, panel_ref, normal_ref, rhs_ref, u_ref, out_ref):
    rhs = total(recv_ref)
    u = dot_t(rhs, pre_ref[...])
    rhs_ref[...] = rhs
    u_ref[...] = u
    put_chunks(out_ref, jnp.dot(u, panel_ref[...], precision=HIGH, preferred_element_type=F32), 2, 0)
    put_chunks(out_ref, jnp.dot(u, normal_ref[...], precision=HIGH, preferred_element_type=F32), 2, 1)


def chunk_kernel(recv_ref, chunk_ref, out_ref):
    k = sum_slot(recv_ref, 2, 0)
    chunk_ref[0] = k
    chunk_ref[1] = sum_slot(recv_ref, 2, 1)
    for s in range(N_FEAT):
        out_ref[s] = k


def normal_kernel(recv_ref, normal_ref, k_ref, out_ref):
    take_chunks(recv_ref, 1, k_ref)
    image = dot_t(k_ref[...], normal_ref[...])
    for i in range(N_EX):
        out_ref[i] = image


def second_kernel(recv_ref, pre_ref, panel_ref, normal_ref, rhs_ref, u_ref, image_ref, v_ref, out_ref):
    image = total(recv_ref)
    v = dot_t(image, pre_ref[...])
    image_ref[...] = image
    v_ref[...] = v
    put_chunks(out_ref, jnp.dot(v, panel_ref[...], precision=HIGH, preferred_element_type=F32), 3, 0)
    put_chunks(out_ref, jnp.dot(v, normal_ref[...], precision=HIGH, preferred_element_type=F32), 3, 1)
    u = u_ref[...]
    row = to_row(jnp.sum(rhs_ref[...] * u, axis=1, keepdims=True), 0)
    row = row + to_row(jnp.sum(u * image, axis=1, keepdims=True), CLASSES)
    row = row + to_row(jnp.sum(v * image, axis=1, keepdims=True), 2 * CLASSES)
    row = jnp.broadcast_to(row, (4, 128))
    for s in range(N_FEAT):
        out_ref[s * 3 + 2] = row


def step_kernel(group_ref, recv_ref, chunk_ref, rhs_ref, u_ref, image_ref, v_ref, scal_ref, out_ref):
    row = sum_slot(recv_ref, 3, 2)[0:1]
    scal_ref[...] = jnp.broadcast_to(row, (8, 128))
    alpha = to_col(row, CLASSES, 0) / to_col(row, CLASSES, CLASSES)
    residual = rhs_ref[...] - alpha * image_ref[...]
    z = u_ref[...] - alpha * v_ref[...]
    rz = to_row(jnp.sum(residual * z, axis=1, keepdims=True))
    alpha_row = to_row(alpha)
    first = group_ref[0] * 4
    mine = iota((4, 128), 1) == iota((4, 128), 0) + first
    alpha_mine = jnp.sum(jnp.where(mine, alpha_row, 0.0), axis=1, keepdims=True)
    kz = chunk_ref[0] - alpha_mine * sum_slot(recv_ref, 3, 0)
    gz = chunk_ref[1] - alpha_mine * sum_slot(recv_ref, 3, 1)
    quad = jnp.sum(kz * gz, axis=1, keepdims=True)
    quad_row = jnp.sum(jnp.where(mine, quad, 0.0), axis=0, keepdims=True)
    which = iota((4, 128), 0)
    tail = jnp.where(which == 0, rz, jnp.where(which == 1, quad_row, 0.0))
    for s in range(N_FEAT):
        out_ref[s * 2] = kz
        out_ref[s * 2 + 1] = tail


def gather_kernel(recv_ref, kz_ref, tail_ref, out_ref):
    take_chunks(recv_ref, 2, kz_ref)
    tail = sum_slot(recv_ref, 2, 1)
    tail_ref[...] = tail
    for i in range(N_EX):
        out_ref[i] = tail[1:2]


def last_kernel(recv_ref, tail_ref, scal_ref, k_ref, kz_ref, out_ref):
    quad = to_col(total(recv_ref), CLASSES)
    rz_next = to_col(tail_ref[0:1, :], CLASSES)
    row = scal_ref[0:1, :]
    rz = to_col(row, CLASSES, 0)
    uu = to_col(row, CLASSES, CLASSES)
    vu = to_col(row, CLASSES, 2 * CLASSES)
    alpha = rz / uu
    beta = rz_next / rz
    cross = uu - alpha * vu
    alpha_next = rz_next / (quad + 2.0 * beta * cross + beta * beta * uu)
    k = k_ref[...]
    out_ref[...] = alpha * k + alpha_next * (kz_ref[...] + beta * k)


def per_device(features, centre_index, labels, precond):
    ex_index = lax.axis_index(EX)
    feat_index = lax.axis_index(FEAT)
    core = lax.axis_index("c")
    local = centre_index[:, 0, :] - ex_index * ROWS
    ft_local = features.T
    ft = lax.all_gather(ft_local, PLANE, axis=0, tiled=True)

    pair = local.reshape(N_PLANE, 2, OWN)
    own_col = jnp.where(core == 0, pair[:, 0], pair[:, 1]).reshape(N_PLANE * OWN, 1)
    other_col = jnp.where(core == 0, pair[:, 1], pair[:, 0]).reshape(N_PLANE * OWN, 1)
    picked = call(pick_kernel, ((N_PLANE, OWN, 2 * SLICE), BF16), ft_local, own_col, other_col, name="pick")
    picked = lax.all_to_all(picked, PLANE, 0, 0, tiled=True)
    spread = call(spread_kernel, ((N_EX, 2 * OWN, WIDTH), BF16), picked, name="spread")
    cen = lax.all_to_all(spread, EX, 0, 0, tiled=True)

    own_rows = lax.dynamic_index_in_dim(local, feat_index, 0, keepdims=False)
    slot = lax.iota(jnp.int32, N_EX)[:, None] == ex_index
    loc = jnp.where(slot, own_rows[None, :], -1).reshape(BLOCK, 1)

    sent = call(other_kernel, ((BLOCK + 8, ROWS), F32), ft, cen, name="other")
    got = lax.ppermute(sent, "c", [(0, 1), (1, 0)])
    dots, squares = call(own_kernel, [((BLOCK, ROWS), F32), ((BLOCK, 128), F32)], ft, cen, name="own")
    panel, normal, part = call(
        panel_kernel,
        [((BLOCK, ROWS), F32), ((BLOCK, ROWS), F32), ((N_EX, CLASSES, BLOCK), F32)],
        dots, squares, sent, got, labels.reshape(1, ROWS), loc, name="panel",
    )
    vec = ((CLASSES, BLOCK), F32)
    part = lax.all_to_all(part, EX, 0, 0, tiled=True)
    rhs, u, part = call(first_kernel, [vec, vec, ((N_FEAT * 2, 4, 128), F32)], part, precond, panel, normal, name="first")
    part = lax.all_to_all(part, FEAT, 0, 0, tiled=True)
    chunk, part = call(chunk_kernel, [((2, 4, 128), F32), ((N_FEAT, 4, 128), F32)], part, name="chunk")
    part = lax.all_to_all(part, FEAT, 0, 0, tiled=True)
    k, part = call(normal_kernel, [((CLASSES, ROWS), F32), ((N_EX, CLASSES, BLOCK), F32)], part, normal, name="normal")
    part = lax.all_to_all(part, EX, 0, 0, tiled=True)
    image, v, part = call(
        second_kernel, [vec, vec, ((N_FEAT * 3, 4, 128), F32)],
        part, precond, panel, normal, rhs, u, name="second",
    )
    part = lax.all_to_all(part, FEAT, 0, 0, tiled=True)
    group = (feat_index // 8).reshape(1)
    scal, part = call(
        step_kernel, [((8, 128), F32), ((N_FEAT * 2, 4, 128), F32)],
        group, part, chunk, rhs, u, image, v, name="step", smem=1,
    )
    part = lax.all_to_all(part, FEAT, 0, 0, tiled=True)
    kz, tail, part = call(
        gather_kernel, [((CLASSES, ROWS), F32), ((4, 128), F32), ((N_EX, 1, 128), F32)], part, name="gather"
    )
    part = lax.all_to_all(part, EX, 0, 0, tiled=True)
    out = call(last_kernel, ((CLASSES, ROWS), F32), part, tail, scal, k, kz, name="last")
    return out.T


def solution(mesh):
    fine = Mesh(mesh.devices.reshape(8, 2, 2, 8, 2), ("z", "xh", "xl", "y", "c"))
    in_specs = (P(EX, FEAT), P(None, EX, None), P(EX), P(FEAT, None))
    return jax.shard_map(per_device, mesh=fine, in_specs=in_specs, out_specs=P(EX, None), check_vma=False)
```

```python
import functools

import jax
import jax.numpy as jnp
from jax import lax
from jax.experimental import pallas as pl
from jax.experimental.pallas import tpu as pltpu
from jax.sharding import Mesh, PartitionSpec as P

CLASSES = 16
GAMMA = 4.0
LAMBDA = 0.05
EPS = 1e-06
HIGH = lax.Precision.HIGHEST
F32 = jnp.float32
BF16 = jnp.bfloat16

ROWS = 1024
BLOCK = 256
OWN = 16
N_EX = 16
N_FEAT = 32
N_PLANE = 16
SLICE = 64
WIDTH = N_PLANE * SLICE
F = 2048
EXAMPLES = ROWS * N_EX

EX = ("z", "xh")
PLANE = ("xl", "y")
FEAT = ("xl", "y", "c")

LANES = (((1,), (1,)), ((), ()))


def dot_t(a, b, precision=HIGH):
    return lax.dot_general(a, b, LANES, precision=precision, preferred_element_type=F32)


def iota(shape, dim):
    return lax.broadcasted_iota(jnp.int32, shape, dim)


def to_row(col, offset=0):
    n = col.shape[0]
    place = iota((n, 128), 1) == iota((n, 128), 0) + offset
    return jnp.sum(jnp.where(place, col, 0.0), axis=0, keepdims=True)


def to_col(row, n, offset=0):
    place = iota((n, 128), 1) == iota((n, 128), 0) + offset
    return jnp.sum(jnp.where(place, row, 0.0), axis=1, keepdims=True)


def call(kernel, outs, *args, name, smem=0, space=pltpu.VMEM):
    spec = [pl.BlockSpec(memory_space=pltpu.SMEM)] * smem
    spec += [pl.BlockSpec(memory_space=pltpu.VMEM)] * (len(args) - smem)
    many = isinstance(outs, list)
    out_spec = pl.BlockSpec(memory_space=pltpu.VMEM)
    return pl.pallas_call(
        kernel,
        out_shape=[pltpu.VMEM(s, d) for s, d in outs] if many else space(*outs),
        in_specs=spec,
        out_specs=[out_spec] * len(outs) if many else out_spec,
        name=name,
        compiler_params=pltpu.CompilerParams(vmem_limit_bytes=12 << 20),
    )(*[x if i < smem else pltpu.with_memory_space_constraint(x, pltpu.VMEM) for i, x in enumerate(args)])


def pick_kernel(ft_ref, own_ref, other_ref, out_ref):
    ft = ft_ref[...]
    zero = jnp.zeros_like(ft)
    n = N_PLANE * OWN
    lane = iota((n, ROWS), 1)

    def chosen(index_ref, table):
        mask = (lane == index_ref[...]).astype(F32).astype(BF16)
        return lax.dot_general(mask, table, LANES, preferred_element_type=F32)

    both = chosen(own_ref, jnp.concatenate([ft, zero], axis=0))
    both = both + chosen(other_ref, jnp.concatenate([zero, ft], axis=0))
    out_ref[...] = both.astype(BF16).reshape(N_PLANE, OWN, 2 * SLICE)


def spread_kernel(side_ref, in_ref, out_ref):
    low = iota((OWN, 128), 1) < SLICE
    half = N_PLANE // 2
    for t in range(half):
        source = 2 * (t % (half // 2)) + half * (side_ref[0] if t < half // 2 else 1 - side_ref[0])
        a = in_ref[source].astype(F32)
        b = in_ref[source + 1].astype(F32)
        own = jnp.where(low, a, pltpu.roll(b, SLICE, 1)).astype(BF16)
        other = jnp.where(low, pltpu.roll(a, SLICE, 1), b).astype(BF16)
        cols = slice(128 * t, 128 * t + 128)
        for i in range(N_EX):
            out_ref[i, 0:OWN, cols] = own
            out_ref[i, OWN : 2 * OWN, cols] = other


def pick_centres(cen_ref, first, half):
    return cen_ref[:, first : first + OWN, half * WIDTH // 2 : (half + 1) * WIDTH // 2].reshape(BLOCK, WIDTH // 2)


def row_squares(ft_ref):
    return jnp.sum(jnp.square(ft_ref[...].astype(F32)), axis=0, keepdims=True)


def near_kernel(ft_ref, cen_ref, other_ref, own_ref, own_sq_ref):
    ft = ft_ref[...]
    other_ref[0:BLOCK, :] = jnp.dot(pick_centres(cen_ref, OWN, 0), ft, preferred_element_type=F32)
    own_ref[...] = jnp.dot(pick_centres(cen_ref, 0, 0), ft, preferred_element_type=F32)

    def squares(first):
        block = cen_ref[:, first : first + OWN, :].reshape(BLOCK, WIDTH).astype(F32)
        return jnp.sum(jnp.square(block), axis=1, keepdims=True)

    other_ref[BLOCK : BLOCK + 8, :] = jnp.zeros((8, ROWS), F32)
    other_ref[BLOCK : BLOCK + 1, :] = row_squares(ft_ref)
    same = iota((BLOCK, BLOCK), 0) == iota((BLOCK, BLOCK), 1)
    other_ref[BLOCK + 1 : BLOCK + 2, 0:BLOCK] = jnp.sum(jnp.where(same, squares(OWN), 0.0), axis=0, keepdims=True)
    own_sq_ref[...] = jnp.broadcast_to(squares(0), (BLOCK, 128))


def other_kernel(ft_ref, cen_ref, near_ref, out_ref):
    block = pick_centres(cen_ref, OWN, 1)
    out_ref[0:BLOCK, :] = near_ref[0:BLOCK, :] + jnp.dot(block, ft_ref[...], preferred_element_type=F32)
    out_ref[BLOCK : BLOCK + 8, :] = near_ref[BLOCK : BLOCK + 8, :]
    out_ref[BLOCK : BLOCK + 1, :] = near_ref[BLOCK : BLOCK + 1, :] + row_squares(ft_ref)


def own_kernel(ft_ref, cen_ref, near_ref, out_ref):
    block = pick_centres(cen_ref, 0, 1)
    out_ref[...] = near_ref[...] + jnp.dot(block, ft_ref[...], preferred_element_type=F32)


def split2(x):
    high = x.astype(BF16)
    return high, (x - high.astype(F32)).astype(BF16)


def split3(x):
    high = x.astype(BF16).astype(F32)
    rest = x - high
    mid = rest.astype(BF16).astype(F32)
    return jnp.concatenate([high, mid, rest - mid], axis=0).astype(BF16)


def fold3(y):
    n = y.shape[0] // 3
    return y[0:n] + (y[n : 2 * n] + y[2 * n : 3 * n])


def panel_kernel(dots_ref, squares_ref, sent_ref, recv_ref, labels_ref, loc_ref, high_ref, low_ref, place_ref, out_ref):
    row_sq = sent_ref[BLOCK : BLOCK + 1, :] + recv_ref[BLOCK : BLOCK + 1, :]
    same = iota((BLOCK, BLOCK), 0) == iota((BLOCK, BLOCK), 1)
    got = jnp.sum(jnp.where(same, recv_ref[BLOCK + 1 : BLOCK + 2, 0:BLOCK], 0.0), axis=1, keepdims=True)
    row_scale = lax.rsqrt(row_sq / F + EPS)
    centre_scale = lax.rsqrt((squares_ref[:, 0:1] + got) / F + EPS)
    dots = dots_ref[...] + recv_ref[0:BLOCK, :]
    cosine = jnp.clip(dots * row_scale * centre_scale, -1.0, 1.0)
    high, low = split2(jnp.exp(GAMMA * (cosine - 1.0)))
    high_ref[...] = high
    low_ref[...] = low
    place_ref[...] = (iota((BLOCK, ROWS), 1) == loc_ref[...]).astype(F32).astype(BF16)
    hit = iota((CLASSES, ROWS), 0) == labels_ref[...]
    targets = jnp.where(hit, CLASSES - 1.0, -1.0).astype(BF16)
    rhs = (dot_t(targets, high, None) + dot_t(targets, low, None)) / EXAMPLES
    for i in range(N_EX):
        out_ref[i] = rhs


def apply_panel(vec, high_ref, low_ref, place_ref):
    parts = split3(vec)

    def times(matrix):
        return fold3(jnp.dot(parts, matrix, preferred_element_type=F32))

    k = times(high_ref[...]) + times(low_ref[...])
    return k, k / EXAMPLES + LAMBDA * times(place_ref[...])


def apply_normal(k, high_ref, low_ref, place_ref):
    parts = split3(k)

    def times(matrix):
        return fold3(dot_t(parts, matrix, None))

    return (times(high_ref[...]) + times(low_ref[...])) / EXAMPLES + LAMBDA * times(place_ref[...])


def total(ref):
    acc = ref[0]
    for i in range(1, ref.shape[0]):
        acc = acc + ref[i]
    return acc


def put_chunks(out_ref, vec, stride, slot):
    for s in range(N_FEAT):
        g, l = s // 8, s % 8
        out_ref[s * stride + slot] = vec[4 * g : 4 * g + 4, 128 * l : 128 * l + 128]


def take_chunks(in_ref, stride, out_ref):
    for s in range(N_FEAT):
        g, l = s // 8, s % 8
        out_ref[4 * g : 4 * g + 4, 128 * l : 128 * l + 128] = in_ref[s * stride]


def sum_slot(ref, stride, slot):
    acc = ref[slot]
    for s in range(1, N_FEAT):
        acc = acc + ref[s * stride + slot]
    return acc


def first_kernel(recv_ref, pre_ref, high_ref, low_ref, place_ref, rhs_ref, u_ref, out_ref):
    rhs = total(recv_ref)
    u = dot_t(rhs, pre_ref[...])
    rhs_ref[...] = rhs
    u_ref[...] = u
    k, g = apply_panel(u, high_ref, low_ref, place_ref)
    put_chunks(out_ref, k, 2, 0)
    put_chunks(out_ref, g, 2, 1)


def chunk_kernel(recv_ref, chunk_ref, out_ref):
    k = sum_slot(recv_ref, 2, 0)
    chunk_ref[0] = k
    chunk_ref[1] = sum_slot(recv_ref, 2, 1)
    for s in range(N_FEAT):
        out_ref[s] = k


def normal_kernel(recv_ref, high_ref, low_ref, place_ref, k_ref, out_ref):
    take_chunks(recv_ref, 1, k_ref)
    image = apply_normal(k_ref[...], high_ref, low_ref, place_ref)
    for i in range(N_EX):
        out_ref[i] = image


def second_kernel(recv_ref, pre_ref, high_ref, low_ref, place_ref, rhs_ref, u_ref, image_ref, v_ref, out_ref):
    image = total(recv_ref)
    v = dot_t(image, pre_ref[...])
    image_ref[...] = image
    v_ref[...] = v
    k, g = apply_panel(v, high_ref, low_ref, place_ref)
    put_chunks(out_ref, k, 3, 0)
    put_chunks(out_ref, g, 3, 1)
    u = u_ref[...]
    row = to_row(jnp.sum(rhs_ref[...] * u, axis=1, keepdims=True), 0)
    row = row + to_row(jnp.sum(u * image, axis=1, keepdims=True), CLASSES)
    row = row + to_row(jnp.sum(v * image, axis=1, keepdims=True), 2 * CLASSES)
    row = jnp.broadcast_to(row, (4, 128))
    for s in range(N_FEAT):
        out_ref[s * 3 + 2] = row


def step_kernel(group_ref, recv_ref, chunk_ref, rhs_ref, u_ref, image_ref, v_ref, scal_ref, out_ref):
    row = sum_slot(recv_ref, 3, 2)[0:1]
    scal_ref[...] = jnp.broadcast_to(row, (8, 128))
    alpha = to_col(row, CLASSES, 0) / to_col(row, CLASSES, CLASSES)
    residual = rhs_ref[...] - alpha * image_ref[...]
    z = u_ref[...] - alpha * v_ref[...]
    rz = to_row(jnp.sum(residual * z, axis=1, keepdims=True))
    alpha_row = to_row(alpha)
    first = group_ref[0] * 4
    mine = iota((4, 128), 1) == iota((4, 128), 0) + first
    alpha_mine = jnp.sum(jnp.where(mine, alpha_row, 0.0), axis=1, keepdims=True)
    kz = chunk_ref[0] - alpha_mine * sum_slot(recv_ref, 3, 0)
    gz = chunk_ref[1] - alpha_mine * sum_slot(recv_ref, 3, 1)
    quad = jnp.sum(kz * gz, axis=1, keepdims=True)
    quad_row = jnp.sum(jnp.where(mine, quad, 0.0), axis=0, keepdims=True)
    which = iota((4, 128), 0)
    tail = jnp.where(which == 0, rz, jnp.where(which == 1, quad_row, 0.0))
    for s in range(N_FEAT):
        out_ref[s * 2] = kz
        out_ref[s * 2 + 1] = tail


def gather_kernel(recv_ref, kz_ref, tail_ref, out_ref):
    take_chunks(recv_ref, 2, kz_ref)
    tail = sum_slot(recv_ref, 2, 1)
    tail_ref[...] = tail
    for i in range(N_EX):
        out_ref[i] = tail[1:2]


def last_kernel(recv_ref, tail_ref, scal_ref, k_ref, kz_ref, out_ref):
    quad = to_col(total(recv_ref), CLASSES)
    rz_next = to_col(tail_ref[0:1, :], CLASSES)
    row = scal_ref[0:1, :]
    rz = to_col(row, CLASSES, 0)
    uu = to_col(row, CLASSES, CLASSES)
    vu = to_col(row, CLASSES, 2 * CLASSES)
    alpha = rz / uu
    beta = rz_next / rz
    cross = uu - alpha * vu
    alpha_next = rz_next / (quad + 2.0 * beta * cross + beta * beta * uu)
    k = k_ref[...]
    out_ref[...] = alpha * k + alpha_next * (kz_ref[...] + beta * k)


def per_device(features, centre_index, labels, precond):
    ex_index = lax.axis_index(EX)
    feat_index = lax.axis_index(FEAT)
    core = lax.axis_index("c")
    local = centre_index[:, 0, :] - ex_index * ROWS
    ft_local = features.T
    near = lax.all_to_all(jnp.broadcast_to(ft_local[None], (8, SLICE, ROWS)), "y", 0, 0, tiled=True)
    near = near.reshape(WIDTH // 2, ROWS)
    far = lax.ppermute(near, "xl", [(0, 1), (1, 0)])

    pair = local.reshape(N_PLANE, 2, OWN)
    own_col = jnp.where(core == 0, pair[:, 0], pair[:, 1]).reshape(N_PLANE * OWN, 1)
    other_col = jnp.where(core == 0, pair[:, 1], pair[:, 0]).reshape(N_PLANE * OWN, 1)
    picked = call(pick_kernel, ((N_PLANE, OWN, 2 * SLICE), BF16), ft_local, own_col, other_col, name="pick")
    picked = lax.all_to_all(picked, PLANE, 0, 0, tiled=True)
    spread = call(spread_kernel, ((N_EX, 2 * OWN, WIDTH), BF16), lax.axis_index("xl").reshape(1), picked, name="spread", smem=1)
    cen = lax.all_to_all(spread, EX, 0, 0, tiled=True)

    own_rows = lax.dynamic_index_in_dim(local, feat_index, 0, keepdims=False)
    slot = lax.iota(jnp.int32, N_EX)[:, None] == ex_index
    loc = jnp.where(slot, own_rows[None, :], -1).reshape(BLOCK, 1)

    dots_t = ((BLOCK, ROWS), F32)
    other, own, own_sq = call(
        near_kernel, [((BLOCK + 8, ROWS), F32), dots_t, ((BLOCK, 128), F32)], near, cen, name="near"
    )
    sent = call(other_kernel, ((BLOCK + 8, ROWS), F32), far, cen, other, name="other")
    got = lax.ppermute(sent, "c", [(0, 1), (1, 0)])
    own = call(own_kernel, dots_t, far, cen, own, name="own")
    half_t = ((BLOCK, ROWS), BF16)
    high, low, place, part = call(
        panel_kernel, [half_t, half_t, half_t, ((N_EX, CLASSES, BLOCK), F32)],
        own, own_sq, sent, got, labels.reshape(1, ROWS), loc, name="panel",
    )
    vec = ((CLASSES, BLOCK), F32)
    part = lax.all_to_all(part, EX, 0, 0, tiled=True)
    rhs, u, part = call(first_kernel, [vec, vec, ((N_FEAT * 2, 4, 128), F32)], part, precond, high, low, place, name="first")
    part = lax.all_to_all(part, FEAT, 0, 0, tiled=True)
    chunk, part = call(chunk_kernel, [((2, 4, 128), F32), ((N_FEAT, 4, 128), F32)], part, name="chunk")
    part = lax.all_to_all(part, FEAT, 0, 0, tiled=True)
    k, part = call(normal_kernel, [((CLASSES, ROWS), F32), ((N_EX, CLASSES, BLOCK), F32)], part, high, low, place, name="normal")
    part = lax.all_to_all(part, EX, 0, 0, tiled=True)
    image, v, part = call(
        second_kernel, [vec, vec, ((N_FEAT * 3, 4, 128), F32)],
        part, precond, high, low, place, rhs, u, name="second",
    )
    part = lax.all_to_all(part, FEAT, 0, 0, tiled=True)
    group = (feat_index // 8).reshape(1)
    scal, part = call(
        step_kernel, [((8, 128), F32), ((N_FEAT * 2, 4, 128), F32)],
        group, part, chunk, rhs, u, image, v, name="step", smem=1,
    )
    part = lax.all_to_all(part, FEAT, 0, 0, tiled=True)
    kz, tail, part = call(
        gather_kernel, [((CLASSES, ROWS), F32), ((4, 128), F32), ((N_EX, 1, 128), F32)], part, name="gather"
    )
    part = lax.all_to_all(part, EX, 0, 0, tiled=True)
    out = call(last_kernel, ((CLASSES, ROWS), F32), part, tail, scal, k, kz, name="last", space=jax.ShapeDtypeStruct)
    return out.T


def solution(mesh):
    fine = Mesh(mesh.devices.reshape(8, 2, 2, 8, 2), ("z", "xh", "xl", "y", "c"))
    in_specs = (P(EX, FEAT), P(None, EX, None), P(EX), P(FEAT, None))
    return jax.shard_map(per_device, mesh=fine, in_specs=in_specs, out_specs=P(EX, None), check_vma=False)
```

```python
import jax
import jax.numpy as jnp
from jax import lax
from jax.experimental import pallas as pl
from jax.experimental.pallas import tpu as pltpu
from jax.sharding import Mesh, PartitionSpec as P


CLASSES = 16
GAMMA = 4.0
LAMBDA = 0.05
EPS = 1e-06
HIGH = lax.Precision.HIGHEST
F32 = jnp.float32
BF16 = jnp.bfloat16

ROWS = 1024
BLOCK = 256
OWN = 16
N_EX = 16
N_FEAT = 32
N_PLANE = 16
SLICE = 64
WIDTH = N_PLANE * SLICE
F = 2048
N_Y = 8
OFFSETS = (0, -1, 1, -2, 2, -3, 3, 4)
EXAMPLES = ROWS * N_EX

EX = ("z", "xh")
PLANE = ("xl", "y")
FEAT = ("xl", "y", "c")

LANES = (((1,), (1,)), ((), ()))


def dot_t(a, b, precision=HIGH):
    return lax.dot_general(a, b, LANES, precision=precision, preferred_element_type=F32)


def iota(shape, dim):
    return lax.broadcasted_iota(jnp.int32, shape, dim)


def to_row(col, offset=0):
    n = col.shape[0]
    place = iota((n, 128), 1) == iota((n, 128), 0) + offset
    return jnp.sum(jnp.where(place, col, 0.0), axis=0, keepdims=True)


def to_col(row, n, offset=0):
    place = iota((n, 128), 1) == iota((n, 128), 0) + offset
    return jnp.sum(jnp.where(place, row, 0.0), axis=1, keepdims=True)


def call(kernel, outs, *args, smem=0, hbm=0, space=pltpu.VMEM, scratch=()):
    vmem = len(args) - smem - hbm
    spaces = [pltpu.SMEM] * smem + [pltpu.VMEM] * vmem + [pl.ANY] * hbm
    args = list(args)
    for i in range(smem, smem + vmem):
        args[i] = pltpu.with_memory_space_constraint(args[i], pltpu.VMEM)
    for i in range(smem + vmem, len(args)):
        args[i] = pltpu.with_memory_space_constraint(args[i], pltpu.HBM)
    many = isinstance(outs, list)
    out_spec = pl.BlockSpec(memory_space=pltpu.VMEM)
    return pl.pallas_call(
        kernel,
        out_shape=[space(s, d) for s, d in outs] if many else space(*outs),
        in_specs=[pl.BlockSpec(memory_space=m) for m in spaces],
        out_specs=[out_spec] * len(outs) if many else out_spec,
        scratch_shapes=scratch,
        compiler_params=pltpu.CompilerParams(vmem_limit_bytes=12 << 20),
    )(*args)


def pick_kernel(ft_ref, own_ref, other_ref, out_ref):
    ft = ft_ref[...]
    zero = jnp.zeros_like(ft)
    n = N_PLANE * OWN
    lane = iota((n, ROWS), 1)

    def chosen(index_ref, table):
        mask = (lane == index_ref[...]).astype(F32).astype(BF16)
        return lax.dot_general(mask, table, LANES, preferred_element_type=F32)

    both = chosen(own_ref, jnp.concatenate([ft, zero], axis=0))
    both = both + chosen(other_ref, jnp.concatenate([zero, ft], axis=0))
    out_ref[...] = both.astype(BF16).reshape(N_PLANE, OWN, 2 * SLICE)


def spread_kernel(place_ref, in_ref, out_ref):
    low = iota((OWN, 128), 1) < SLICE
    side, y = place_ref[0], place_ref[1]
    for t, offset in enumerate(OFFSETS):
        row = lax.rem(y + (offset + N_Y), N_Y)
        a = in_ref[side * N_Y + row].astype(F32)
        b = in_ref[(1 - side) * N_Y + row].astype(F32)
        own = jnp.where(low, a, pltpu.roll(b, SLICE, 1)).astype(BF16)
        other = jnp.where(low, pltpu.roll(a, SLICE, 1), b).astype(BF16)
        cols = slice(128 * t, 128 * t + 128)
        for i in range(N_EX):
            out_ref[i, 0:OWN, cols] = own
            out_ref[i, OWN : 2 * OWN, cols] = other


def diagonal():
    return iota((BLOCK, BLOCK), 0) == iota((BLOCK, BLOCK), 1)


def half_dots(ft, cen_ref, first):
    block = cen_ref[:, first : first + OWN, :].reshape(BLOCK, WIDTH)
    squares = jnp.sum(jnp.square(block.astype(F32)), axis=1, keepdims=True)
    squares = jnp.sum(jnp.where(diagonal(), squares, 0.0), axis=0, keepdims=True)
    return jnp.dot(block, ft, preferred_element_type=F32), squares


def dots_kernel(near_ref, far_ref, cen_ref, *refs):
    *chunk_hbm, out_ref, dots_ref, squares_ref, ft_ref, sems = refs
    copies = []
    for i, chunk in enumerate(chunk_hbm):
        copies.append(pltpu.make_async_copy(chunk, ft_ref.at[128 * i : 128 * i + 128], sems.at[i]))
        copies[-1].start()
    first = 128 * len(chunk_hbm)
    ft_ref[first : first + SLICE] = near_ref[...]
    ft_ref[first + SLICE : first + 2 * SLICE] = far_ref[...]

    def squares(start):
        return jnp.sum(jnp.square(ft_ref[start : start + 128].astype(F32)), axis=0, keepdims=True)

    row_sq = squares(first)
    for i, copy in enumerate(copies):
        copy.wait()
        row_sq += squares(128 * i)
    out_ref[BLOCK : BLOCK + 8, :] = jnp.zeros((8, ROWS), F32)
    out_ref[BLOCK : BLOCK + 1, :] = row_sq
    ft = ft_ref[...]
    dots, squares = half_dots(ft, cen_ref, OWN)
    out_ref[0:BLOCK, :] = dots
    out_ref[BLOCK + 1 : BLOCK + 2, 0:BLOCK] = squares
    dots, squares = half_dots(ft, cen_ref, 0)
    dots_ref[...] = dots
    squares_ref[...] = jnp.broadcast_to(squares, (8, BLOCK))


def split2(x):
    high = x.astype(BF16)
    return high, (x - high.astype(F32)).astype(BF16)


def split3(x):
    high = x.astype(BF16).astype(F32)
    rest = x - high
    mid = rest.astype(BF16).astype(F32)
    return jnp.concatenate([high, mid, rest - mid], axis=0).astype(BF16)


def fold3(y):
    n = y.shape[0] // 3
    return y[0:n] + (y[n : 2 * n] + y[2 * n : 3 * n])


def panel_kernel(
    dots_ref, squares_ref, sent_ref, labels_ref, loc_ref, recv_hbm, high_ref, low_ref, place_ref, out_ref, recv_ref, sem
):
    copy = pltpu.make_async_copy(recv_hbm, recv_ref, sem)
    copy.start()
    place_ref[...] = (iota((BLOCK, ROWS), 1) == loc_ref[...]).astype(F32).astype(BF16)
    hit = iota((CLASSES, ROWS), 0) == labels_ref[...]
    targets = jnp.where(hit, CLASSES - 1.0, -1.0).astype(BF16)
    copy.wait()
    row_sq = sent_ref[BLOCK : BLOCK + 1, :] + recv_ref[BLOCK : BLOCK + 1, :]
    centre_sq = squares_ref[0:1, :] + recv_ref[BLOCK + 1 : BLOCK + 2, 0:BLOCK]
    centre_sq = jnp.sum(jnp.where(diagonal(), centre_sq, 0.0), axis=1, keepdims=True)
    row_scale = lax.rsqrt(row_sq / F + EPS)
    centre_scale = lax.rsqrt(centre_sq / F + EPS)
    dots = dots_ref[...] + recv_ref[0:BLOCK, :]
    cosine = jnp.clip(dots * row_scale * centre_scale, -1.0, 1.0)
    high, low = split2(jnp.exp(GAMMA * (cosine - 1.0)))
    high_ref[...] = high
    low_ref[...] = low
    rhs = (dot_t(targets, high, None) + dot_t(targets, low, None)) / EXAMPLES
    for i in range(N_EX):
        out_ref[i] = rhs


def apply_panel(vec, high_ref, low_ref, place_ref):
    parts = split3(vec)

    def times(matrix):
        return fold3(jnp.dot(parts, matrix, preferred_element_type=F32))

    k = times(high_ref[...]) + times(low_ref[...])
    return k, k / EXAMPLES + LAMBDA * times(place_ref[...])


def apply_normal(k, high_ref, low_ref, place_ref):
    parts = split3(k)

    def times(matrix):
        return fold3(dot_t(parts, matrix, None))

    return (times(high_ref[...]) + times(low_ref[...])) / EXAMPLES + LAMBDA * times(place_ref[...])


def total(ref):
    acc = ref[0]
    for i in range(1, ref.shape[0]):
        acc = acc + ref[i]
    return acc


def put_chunks(out_ref, vec, stride, slot):
    for s in range(N_FEAT):
        g, l = s // 8, s % 8
        out_ref[s * stride + slot] = vec[4 * g : 4 * g + 4, 128 * l : 128 * l + 128]


def take_chunks(in_ref, stride, out_ref):
    for s in range(N_FEAT):
        g, l = s // 8, s % 8
        out_ref[4 * g : 4 * g + 4, 128 * l : 128 * l + 128] = in_ref[s * stride]


def sum_slot(ref, stride, slot):
    acc = ref[slot]
    for s in range(1, N_FEAT):
        acc = acc + ref[s * stride + slot]
    return acc


def first_kernel(recv_ref, pre_ref, high_ref, low_ref, place_ref, rhs_ref, u_ref, out_ref):
    rhs = total(recv_ref)
    u = dot_t(rhs, pre_ref[...])
    rhs_ref[...] = rhs
    u_ref[...] = u
    k, g = apply_panel(u, high_ref, low_ref, place_ref)
    put_chunks(out_ref, k, 2, 0)
    put_chunks(out_ref, g, 2, 1)


def chunk_kernel(recv_ref, chunk_ref, out_ref):
    k = sum_slot(recv_ref, 2, 0)
    chunk_ref[0] = k
    chunk_ref[1] = sum_slot(recv_ref, 2, 1)
    for s in range(N_FEAT):
        out_ref[s] = k


def normal_kernel(recv_ref, high_ref, low_ref, place_ref, k_ref, out_ref):
    take_chunks(recv_ref, 1, k_ref)
    image = apply_normal(k_ref[...], high_ref, low_ref, place_ref)
    for i in range(N_EX):
        out_ref[i] = image


def second_kernel(recv_ref, pre_ref, high_ref, low_ref, place_ref, rhs_ref, u_ref, image_ref, v_ref, out_ref):
    image = total(recv_ref)
    v = dot_t(image, pre_ref[...])
    image_ref[...] = image
    v_ref[...] = v
    k, g = apply_panel(v, high_ref, low_ref, place_ref)
    put_chunks(out_ref, k, 3, 0)
    put_chunks(out_ref, g, 3, 1)
    u = u_ref[...]
    row = to_row(jnp.sum(rhs_ref[...] * u, axis=1, keepdims=True), 0)
    row = row + to_row(jnp.sum(u * image, axis=1, keepdims=True), CLASSES)
    row = row + to_row(jnp.sum(v * image, axis=1, keepdims=True), 2 * CLASSES)
    row = jnp.broadcast_to(row, (4, 128))
    for s in range(N_FEAT):
        out_ref[s * 3 + 2] = row


def step_kernel(group_ref, recv_ref, chunk_ref, rhs_ref, u_ref, image_ref, v_ref, scal_ref, out_ref):
    row = sum_slot(recv_ref, 3, 2)[0:1]
    scal_ref[...] = jnp.broadcast_to(row, (8, 128))
    alpha = to_col(row, CLASSES, 0) / to_col(row, CLASSES, CLASSES)
    residual = rhs_ref[...] - alpha * image_ref[...]
    z = u_ref[...] - alpha * v_ref[...]
    rz = to_row(jnp.sum(residual * z, axis=1, keepdims=True))
    alpha_row = to_row(alpha)
    first = group_ref[0] * 4
    mine = iota((4, 128), 1) == iota((4, 128), 0) + first
    alpha_mine = jnp.sum(jnp.where(mine, alpha_row, 0.0), axis=1, keepdims=True)
    kz = chunk_ref[0] - alpha_mine * sum_slot(recv_ref, 3, 0)
    gz = chunk_ref[1] - alpha_mine * sum_slot(recv_ref, 3, 1)
    quad = jnp.sum(kz * gz, axis=1, keepdims=True)
    quad_row = jnp.sum(jnp.where(mine, quad, 0.0), axis=0, keepdims=True)
    which = iota((4, 128), 0)
    tail = jnp.where(which == 0, rz, jnp.where(which == 1, quad_row, 0.0))
    for s in range(N_FEAT):
        out_ref[s * 2] = kz
        out_ref[s * 2 + 1] = tail


def gather_kernel(recv_ref, kz_ref, tail_ref, out_ref):
    take_chunks(recv_ref, 2, kz_ref)
    tail = sum_slot(recv_ref, 2, 1)
    tail_ref[...] = tail
    for i in range(N_EX):
        out_ref[i] = tail[1:2]


def last_kernel(recv_ref, tail_ref, scal_ref, k_ref, kz_ref, out_ref):
    quad = to_col(total(recv_ref), CLASSES)
    rz_next = to_col(tail_ref[0:1, :], CLASSES)
    row = scal_ref[0:1, :]
    rz = to_col(row, CLASSES, 0)
    uu = to_col(row, CLASSES, CLASSES)
    vu = to_col(row, CLASSES, 2 * CLASSES)
    alpha = rz / uu
    beta = rz_next / rz
    cross = uu - alpha * vu
    alpha_next = rz_next / (quad + 2.0 * beta * cross + beta * beta * uu)
    k = k_ref[...]
    out_ref[...] = alpha * k + alpha_next * (kz_ref[...] + beta * k)


def predict(features, centre_index, labels, precond):
    ex_index = lax.axis_index(EX)
    feat_index = lax.axis_index(FEAT)
    core = lax.axis_index("c")
    local = centre_index[:, 0, :] - ex_index * ROWS
    ft_local = features.T
    swapped = lax.ppermute(ft_local, "xl", [(0, 1), (1, 0)])
    here = jnp.concatenate([ft_local, swapped], axis=0)
    up = [(i, (i + 1) % N_Y) for i in range(N_Y)]
    down = [(i, (i - 1) % N_Y) for i in range(N_Y)]
    chunks = [here]
    below = above = here
    for _ in range(3):
        below = lax.ppermute(below, "y", up)
        above = lax.ppermute(above, "y", down)
        chunks += [below, above]
    chunks += [lax.ppermute(below[:SLICE], "y", up), lax.ppermute(above[SLICE:], "y", down)]

    pair = local.reshape(N_PLANE, 2, OWN)
    own_col = jnp.where(core == 0, pair[:, 0], pair[:, 1]).reshape(N_PLANE * OWN, 1)
    other_col = jnp.where(core == 0, pair[:, 1], pair[:, 0]).reshape(N_PLANE * OWN, 1)
    picked = call(pick_kernel, ((N_PLANE, OWN, 2 * SLICE), BF16), ft_local, own_col, other_col)
    picked = lax.all_to_all(picked, PLANE, 0, 0, tiled=True)
    spread = call(spread_kernel, ((N_EX, 2 * OWN, WIDTH), BF16), jnp.stack([lax.axis_index("xl"), lax.axis_index("y")]), picked, smem=1)
    cen = lax.all_to_all(spread, EX, 0, 0, tiled=True)

    own_rows = lax.dynamic_index_in_dim(local, feat_index, 0, keepdims=False)
    slot = lax.iota(jnp.int32, N_EX)[:, None] == ex_index
    loc = jnp.where(slot, own_rows[None, :], -1).reshape(BLOCK, 1)

    dots_t = ((BLOCK, ROWS), F32)
    sent, own, own_sq = call(
        dots_kernel, [((BLOCK + 8, ROWS), F32), dots_t, ((8, BLOCK), F32)], *chunks[-2:], cen, *chunks[:-2],
        hbm=len(chunks) - 2,
        scratch=[pltpu.VMEM((WIDTH, ROWS), BF16), pltpu.SemaphoreType.DMA((len(chunks) - 2,))],
    )
    got = lax.ppermute(sent, "c", [(0, 1), (1, 0)])
    half_t = ((BLOCK, ROWS), BF16)
    high, low, place, part = call(
        panel_kernel, [half_t, half_t, half_t, ((N_EX, CLASSES, BLOCK), F32)],
        own, own_sq, sent, labels.reshape(1, ROWS), loc, got, hbm=1,
        scratch=[pltpu.VMEM(sent.shape, F32), pltpu.SemaphoreType.DMA],
    )
    vec = ((CLASSES, BLOCK), F32)
    part = lax.all_to_all(part, EX, 0, 0, tiled=True)
    rhs, u, part = call(first_kernel, [vec, vec, ((N_FEAT * 2, 4, 128), F32)], part, precond, high, low, place)
    part = lax.all_to_all(part, FEAT, 0, 0, tiled=True)
    chunk, part = call(chunk_kernel, [((2, 4, 128), F32), ((N_FEAT, 4, 128), F32)], part)
    part = lax.all_to_all(part, FEAT, 0, 0, tiled=True)
    k, part = call(normal_kernel, [((CLASSES, ROWS), F32), ((N_EX, CLASSES, BLOCK), F32)], part, high, low, place)
    part = lax.all_to_all(part, EX, 0, 0, tiled=True)
    image, v, part = call(
        second_kernel, [vec, vec, ((N_FEAT * 3, 4, 128), F32)],
        part, precond, high, low, place, rhs, u,
    )
    part = lax.all_to_all(part, FEAT, 0, 0, tiled=True)
    group = (feat_index // 8).reshape(1)
    scal, part = call(
        step_kernel, [((8, 128), F32), ((N_FEAT * 2, 4, 128), F32)],
        group, part, chunk, rhs, u, image, v, smem=1,
    )
    part = lax.all_to_all(part, FEAT, 0, 0, tiled=True)
    kz, tail, part = call(gather_kernel, [((CLASSES, ROWS), F32), ((4, 128), F32), ((N_EX, 1, 128), F32)], part)
    part = lax.all_to_all(part, EX, 0, 0, tiled=True)
    out = call(last_kernel, ((CLASSES, ROWS), F32), part, tail, scal, k, kz, space=jax.ShapeDtypeStruct)
    return out.T


def solution(mesh):
    fine = Mesh(mesh.devices.reshape(8, 2, 2, 8, 2), ("z", "xh", "xl", "y", "c"))
    in_specs = (P(EX, FEAT), P(None, EX, None), P(EX), P(FEAT, None))
    return jax.shard_map(predict, mesh=fine, in_specs=in_specs, out_specs=P(EX, None), check_vma=False)
```

```python
import jax
import jax.numpy as jnp
from jax import lax
from jax.experimental import pallas as pl
from jax.experimental.pallas import tpu as pltpu
from jax.sharding import Mesh, PartitionSpec as P


CLASSES = 16
GAMMA = 4.0
LAMBDA = 0.05
EPS = 1e-06
HIGH = lax.Precision.HIGHEST
F32 = jnp.float32
BF16 = jnp.bfloat16

ROWS = 1024
BLOCK = 256
OWN = 16
N_EX = 16
N_FEAT = 32
N_PLANE = 16
SLICE = 64
WIDTH = N_PLANE * SLICE
F = 2048
N_Y = 8
OFFSETS = (0, 4, -1, 1, -2, 2, -3, 3)
EXAMPLES = ROWS * N_EX

EX = ("z", "xh")
PLANE = ("xl", "y")
FEAT = ("xl", "y", "c")

LANES = (((1,), (1,)), ((), ()))


def dot_t(a, b, precision=HIGH):
    return lax.dot_general(a, b, LANES, precision=precision, preferred_element_type=F32)


def iota(shape, dim):
    return lax.broadcasted_iota(jnp.int32, shape, dim)


def to_row(col, offset=0):
    n = col.shape[0]
    place = iota((n, 128), 1) == iota((n, 128), 0) + offset
    return jnp.sum(jnp.where(place, col, 0.0), axis=0, keepdims=True)


def to_col(row, n, offset=0):
    place = iota((n, 128), 1) == iota((n, 128), 0) + offset
    return jnp.sum(jnp.where(place, row, 0.0), axis=1, keepdims=True)


def call(kernel, outs, *args, smem=0, hbm=0, space=pltpu.VMEM, scratch=()):
    vmem = len(args) - smem - hbm
    spaces = [pltpu.SMEM] * smem + [pltpu.VMEM] * vmem + [pl.ANY] * hbm
    args = list(args)
    for i in range(smem, smem + vmem):
        args[i] = pltpu.with_memory_space_constraint(args[i], pltpu.VMEM)
    for i in range(smem + vmem, len(args)):
        args[i] = pltpu.with_memory_space_constraint(args[i], pltpu.HBM)
    many = isinstance(outs, list)
    out_spec = pl.BlockSpec(memory_space=pltpu.VMEM)
    return pl.pallas_call(
        kernel,
        out_shape=[space(s, d) for s, d in outs] if many else space(*outs),
        in_specs=[pl.BlockSpec(memory_space=m) for m in spaces],
        out_specs=[out_spec] * len(outs) if many else out_spec,
        scratch_shapes=scratch,
        compiler_params=pltpu.CompilerParams(vmem_limit_bytes=12 << 20),
    )(*args)


def pick_kernel(ft_ref, own_ref, other_ref, out_ref):
    ft = ft_ref[...]
    zero = jnp.zeros_like(ft)
    n = N_PLANE * OWN
    lane = iota((n, ROWS), 1)

    def chosen(index_ref, table):
        mask = (lane == index_ref[...]).astype(F32).astype(BF16)
        return lax.dot_general(mask, table, LANES, preferred_element_type=F32)

    both = chosen(own_ref, jnp.concatenate([ft, zero], axis=0))
    both = both + chosen(other_ref, jnp.concatenate([zero, ft], axis=0))
    out_ref[...] = both.astype(BF16).reshape(N_PLANE, OWN, 2 * SLICE)


def spread_kernel(place_ref, in_ref, out_ref):
    low = iota((OWN, 128), 1) < SLICE
    side, y = place_ref[0], place_ref[1]
    for t, offset in enumerate(OFFSETS):
        row = lax.rem(y + (offset + N_Y), N_Y)
        a = in_ref[side * N_Y + row].astype(F32)
        b = in_ref[(1 - side) * N_Y + row].astype(F32)
        own = jnp.where(low, a, pltpu.roll(b, SLICE, 1)).astype(BF16)
        other = jnp.where(low, pltpu.roll(a, SLICE, 1), b).astype(BF16)
        cols = slice(128 * t, 128 * t + 128)
        for i in range(N_EX):
            out_ref[i, 0:OWN, cols] = own
            out_ref[i, OWN : 2 * OWN, cols] = other


def diagonal():
    return iota((BLOCK, BLOCK), 0) == iota((BLOCK, BLOCK), 1)


def half_dots(ft, cen_ref, first):
    block = cen_ref[:, first : first + OWN, :].reshape(BLOCK, WIDTH)
    squares = jnp.sum(jnp.square(block.astype(F32)), axis=1, keepdims=True)
    squares = jnp.sum(jnp.where(diagonal(), squares, 0.0), axis=0, keepdims=True)
    return jnp.dot(block, ft, preferred_element_type=F32), squares


def dots_kernel(cen_ref, *refs):
    *chunk_hbm, out_ref, dots_ref, squares_ref, ft_ref, sems = refs
    copies = []
    for i, chunk in enumerate(chunk_hbm):
        copies.append(pltpu.make_async_copy(chunk, ft_ref.at[128 * i : 128 * i + 128], sems.at[i]))
        copies[-1].start()

    def squares(start):
        return jnp.sum(jnp.square(ft_ref[start : start + 128].astype(F32)), axis=0, keepdims=True)

    row_sq = jnp.zeros((1, ROWS), F32)
    for i, copy in enumerate(copies):
        copy.wait()
        row_sq += squares(128 * i)
    out_ref[BLOCK : BLOCK + 8, :] = jnp.zeros((8, ROWS), F32)
    out_ref[BLOCK : BLOCK + 1, :] = row_sq
    ft = ft_ref[...]
    dots, squares = half_dots(ft, cen_ref, OWN)
    out_ref[0:BLOCK, :] = dots
    out_ref[BLOCK + 1 : BLOCK + 2, 0:BLOCK] = squares
    dots, squares = half_dots(ft, cen_ref, 0)
    dots_ref[...] = dots
    squares_ref[...] = jnp.broadcast_to(squares, (8, BLOCK))


def split2(x):
    high = x.astype(BF16)
    return high, (x - high.astype(F32)).astype(BF16)


def split3(x):
    high = x.astype(BF16).astype(F32)
    rest = x - high
    mid = rest.astype(BF16).astype(F32)
    return jnp.concatenate([high, mid, rest - mid], axis=0).astype(BF16)


def fold3(y):
    n = y.shape[0] // 3
    return y[0:n] + (y[n : 2 * n] + y[2 * n : 3 * n])


def panel_kernel(
    dots_ref, squares_ref, sent_ref, labels_ref, loc_ref, recv_hbm, high_ref, low_ref, place_ref, out_ref, recv_ref, sem
):
    copy = pltpu.make_async_copy(recv_hbm, recv_ref, sem)
    copy.start()
    place_ref[...] = (iota((BLOCK, ROWS), 1) == loc_ref[...]).astype(F32).astype(BF16)
    hit = iota((CLASSES, ROWS), 0) == labels_ref[...]
    targets = jnp.where(hit, CLASSES - 1.0, -1.0).astype(BF16)
    copy.wait()
    row_sq = sent_ref[BLOCK : BLOCK + 1, :] + recv_ref[BLOCK : BLOCK + 1, :]
    centre_sq = squares_ref[0:1, :] + recv_ref[BLOCK + 1 : BLOCK + 2, 0:BLOCK]
    centre_sq = jnp.sum(jnp.where(diagonal(), centre_sq, 0.0), axis=1, keepdims=True)
    row_scale = lax.rsqrt(row_sq / F + EPS)
    centre_scale = lax.rsqrt(centre_sq / F + EPS)
    dots = dots_ref[...] + recv_ref[0:BLOCK, :]
    cosine = jnp.clip(dots * row_scale * centre_scale, -1.0, 1.0)
    high, low = split2(jnp.exp(GAMMA * (cosine - 1.0)))
    high_ref[...] = high
    low_ref[...] = low
    rhs = (dot_t(targets, high, None) + dot_t(targets, low, None)) / EXAMPLES
    for i in range(N_EX):
        out_ref[i] = rhs


def apply_panel(vec, high_ref, low_ref, place_ref):
    parts = split3(vec)

    def times(matrix):
        return fold3(jnp.dot(parts, matrix, preferred_element_type=F32))

    k = times(high_ref[...]) + times(low_ref[...])
    return k, k / EXAMPLES + LAMBDA * times(place_ref[...])


def apply_normal(k, high_ref, low_ref, place_ref):
    parts = split3(k)

    def times(matrix):
        return fold3(dot_t(parts, matrix, None))

    return (times(high_ref[...]) + times(low_ref[...])) / EXAMPLES + LAMBDA * times(place_ref[...])


def total(ref):
    acc = ref[0]
    for i in range(1, ref.shape[0]):
        acc = acc + ref[i]
    return acc


def put_chunks(out_ref, vec, stride, slot):
    for s in range(N_FEAT):
        g, l = s // 8, s % 8
        out_ref[s * stride + slot] = vec[4 * g : 4 * g + 4, 128 * l : 128 * l + 128]


def take_chunks(in_ref, stride, out_ref):
    for s in range(N_FEAT):
        g, l = s // 8, s % 8
        out_ref[4 * g : 4 * g + 4, 128 * l : 128 * l + 128] = in_ref[s * stride]


def sum_slot(ref, stride, slot):
    acc = ref[slot]
    for s in range(1, N_FEAT):
        acc = acc + ref[s * stride + slot]
    return acc


def first_kernel(recv_ref, pre_ref, high_ref, low_ref, place_ref, rhs_ref, u_ref, out_ref):
    rhs = total(recv_ref)
    u = dot_t(rhs, pre_ref[...])
    rhs_ref[...] = rhs
    u_ref[...] = u
    k, g = apply_panel(u, high_ref, low_ref, place_ref)
    put_chunks(out_ref, k, 2, 0)
    put_chunks(out_ref, g, 2, 1)


def chunk_kernel(recv_ref, chunk_ref, out_ref):
    k = sum_slot(recv_ref, 2, 0)
    chunk_ref[0] = k
    chunk_ref[1] = sum_slot(recv_ref, 2, 1)
    for s in range(N_FEAT):
        out_ref[s] = k


def normal_kernel(recv_ref, high_ref, low_ref, place_ref, k_ref, out_ref):
    take_chunks(recv_ref, 1, k_ref)
    image = apply_normal(k_ref[...], high_ref, low_ref, place_ref)
    for i in range(N_EX):
        out_ref[i] = image


def second_kernel(recv_ref, pre_ref, high_ref, low_ref, place_ref, rhs_ref, u_ref, image_ref, v_ref, out_ref):
    image = total(recv_ref)
    v = dot_t(image, pre_ref[...])
    image_ref[...] = image
    v_ref[...] = v
    k, g = apply_panel(v, high_ref, low_ref, place_ref)
    put_chunks(out_ref, k, 3, 0)
    put_chunks(out_ref, g, 3, 1)
    u = u_ref[...]
    row = to_row(jnp.sum(rhs_ref[...] * u, axis=1, keepdims=True), 0)
    row = row + to_row(jnp.sum(u * image, axis=1, keepdims=True), CLASSES)
    row = row + to_row(jnp.sum(v * image, axis=1, keepdims=True), 2 * CLASSES)
    row = jnp.broadcast_to(row, (4, 128))
    for s in range(N_FEAT):
        out_ref[s * 3 + 2] = row


def step_kernel(group_ref, recv_ref, chunk_ref, rhs_ref, u_ref, image_ref, v_ref, scal_ref, out_ref):
    row = sum_slot(recv_ref, 3, 2)[0:1]
    scal_ref[...] = jnp.broadcast_to(row, (8, 128))
    alpha = to_col(row, CLASSES, 0) / to_col(row, CLASSES, CLASSES)
    residual = rhs_ref[...] - alpha * image_ref[...]
    z = u_ref[...] - alpha * v_ref[...]
    rz = to_row(jnp.sum(residual * z, axis=1, keepdims=True))
    alpha_row = to_row(alpha)
    first = group_ref[0] * 4
    mine = iota((4, 128), 1) == iota((4, 128), 0) + first
    alpha_mine = jnp.sum(jnp.where(mine, alpha_row, 0.0), axis=1, keepdims=True)
    kz = chunk_ref[0] - alpha_mine * sum_slot(recv_ref, 3, 0)
    gz = chunk_ref[1] - alpha_mine * sum_slot(recv_ref, 3, 1)
    quad = jnp.sum(kz * gz, axis=1, keepdims=True)
    quad_row = jnp.sum(jnp.where(mine, quad, 0.0), axis=0, keepdims=True)
    which = iota((4, 128), 0)
    tail = jnp.where(which == 0, rz, jnp.where(which == 1, quad_row, 0.0))
    for s in range(N_FEAT):
        out_ref[s * 2] = kz
        out_ref[s * 2 + 1] = tail


def gather_kernel(recv_ref, kz_ref, tail_ref, out_ref):
    take_chunks(recv_ref, 2, kz_ref)
    tail = sum_slot(recv_ref, 2, 1)
    tail_ref[...] = tail
    for i in range(N_EX):
        out_ref[i] = tail[1:2]


def last_kernel(recv_ref, tail_ref, scal_ref, k_ref, kz_ref, out_ref):
    quad = to_col(total(recv_ref), CLASSES)
    rz_next = to_col(tail_ref[0:1, :], CLASSES)
    row = scal_ref[0:1, :]
    rz = to_col(row, CLASSES, 0)
    uu = to_col(row, CLASSES, CLASSES)
    vu = to_col(row, CLASSES, 2 * CLASSES)
    alpha = rz / uu
    beta = rz_next / rz
    cross = uu - alpha * vu
    alpha_next = rz_next / (quad + 2.0 * beta * cross + beta * beta * uu)
    k = k_ref[...]
    out_ref[...] = alpha * k + alpha_next * (kz_ref[...] + beta * k)


def predict(features, centre_index, labels, precond):
    ex_index = lax.axis_index(EX)
    feat_index = lax.axis_index(FEAT)
    core = lax.axis_index("c")
    local = centre_index[:, 0, :] - ex_index * ROWS
    ft_local = features.T
    swapped = lax.ppermute(ft_local, "xl", [(0, 1), (1, 0)])
    here = jnp.concatenate([ft_local, swapped], axis=0)
    up = [(i, (i + 1) % N_Y) for i in range(N_Y)]
    down = [(i, (i - 1) % N_Y) for i in range(N_Y)]
    chunks = [here]
    below = above = here
    for _ in range(3):
        below = lax.ppermute(below, "y", up)
        above = lax.ppermute(above, "y", down)
        chunks += [below, above]
    chunks.insert(1, lax.ppermute(here, "y", [(i, (i + N_Y // 2) % N_Y) for i in range(N_Y)]))

    pair = local.reshape(N_PLANE, 2, OWN)
    own_col = jnp.where(core == 0, pair[:, 0], pair[:, 1]).reshape(N_PLANE * OWN, 1)
    other_col = jnp.where(core == 0, pair[:, 1], pair[:, 0]).reshape(N_PLANE * OWN, 1)
    picked = call(pick_kernel, ((N_PLANE, OWN, 2 * SLICE), BF16), ft_local, own_col, other_col)
    picked = lax.all_to_all(picked, PLANE, 0, 0, tiled=True)
    spread = call(spread_kernel, ((N_EX, 2 * OWN, WIDTH), BF16), jnp.stack([lax.axis_index("xl"), lax.axis_index("y")]), picked, smem=1)
    cen = lax.all_to_all(spread, EX, 0, 0, tiled=True)

    own_rows = lax.dynamic_index_in_dim(local, feat_index, 0, keepdims=False)
    slot = lax.iota(jnp.int32, N_EX)[:, None] == ex_index
    loc = jnp.where(slot, own_rows[None, :], -1).reshape(BLOCK, 1)

    dots_t = ((BLOCK, ROWS), F32)
    sent, own, own_sq = call(
        dots_kernel, [((BLOCK + 8, ROWS), F32), dots_t, ((8, BLOCK), F32)], cen, *chunks, hbm=len(chunks),
        scratch=[pltpu.VMEM((WIDTH, ROWS), BF16), pltpu.SemaphoreType.DMA((len(chunks),))],
    )
    got = lax.ppermute(sent, "c", [(0, 1), (1, 0)])
    half_t = ((BLOCK, ROWS), BF16)
    high, low, place, part = call(
        panel_kernel, [half_t, half_t, half_t, ((N_EX, CLASSES, BLOCK), F32)],
        own, own_sq, sent, labels.reshape(1, ROWS), loc, got, hbm=1,
        scratch=[pltpu.VMEM(sent.shape, F32), pltpu.SemaphoreType.DMA],
    )
    vec = ((CLASSES, BLOCK), F32)
    part = lax.all_to_all(part, EX, 0, 0, tiled=True)
    rhs, u, part = call(first_kernel, [vec, vec, ((N_FEAT * 2, 4, 128), F32)], part, precond, high, low, place)
    part = lax.all_to_all(part, FEAT, 0, 0, tiled=True)
    chunk, part = call(chunk_kernel, [((2, 4, 128), F32), ((N_FEAT, 4, 128), F32)], part)
    part = lax.all_to_all(part, FEAT, 0, 0, tiled=True)
    k, part = call(normal_kernel, [((CLASSES, ROWS), F32), ((N_EX, CLASSES, BLOCK), F32)], part, high, low, place)
    part = lax.all_to_all(part, EX, 0, 0, tiled=True)
    image, v, part = call(
        second_kernel, [vec, vec, ((N_FEAT * 3, 4, 128), F32)],
        part, precond, high, low, place, rhs, u,
    )
    part = lax.all_to_all(part, FEAT, 0, 0, tiled=True)
    group = (feat_index // 8).reshape(1)
    scal, part = call(
        step_kernel, [((8, 128), F32), ((N_FEAT * 2, 4, 128), F32)],
        group, part, chunk, rhs, u, image, v, smem=1,
    )
    part = lax.all_to_all(part, FEAT, 0, 0, tiled=True)
    kz, tail, part = call(gather_kernel, [((CLASSES, ROWS), F32), ((4, 128), F32), ((N_EX, 1, 128), F32)], part)
    part = lax.all_to_all(part, EX, 0, 0, tiled=True)
    out = call(last_kernel, ((CLASSES, ROWS), F32), part, tail, scal, k, kz, space=jax.ShapeDtypeStruct)
    return out.T


def solution(mesh):
    fine = Mesh(mesh.devices.reshape(8, 2, 2, 8, 2), ("z", "xh", "xl", "y", "c"))
    in_specs = (P(EX, FEAT), P(None, EX, None), P(EX), P(FEAT, None))
    return jax.shard_map(predict, mesh=fine, in_specs=in_specs, out_specs=P(EX, None), check_vma=False)
```

```python
import jax
import jax.numpy as jnp
from jax import lax
from jax.experimental import pallas as pl
from jax.experimental.pallas import tpu as pltpu
from jax.sharding import Mesh, PartitionSpec as P


CLASSES = 16
GAMMA = 4.0
LAMBDA = 0.05
EPS = 1e-06
HIGH = lax.Precision.HIGHEST
F32 = jnp.float32
BF16 = jnp.bfloat16

ROWS = 1024
BLOCK = 256
OWN = 16
N_EX = 16
N_FEAT = 32
N_PLANE = 16
SLICE = 64
WIDTH = N_PLANE * SLICE
F = 2048
N_Y = 8
OFFSETS = (0, -1, 1, -2, 2, -3, 3, 4)
EXAMPLES = ROWS * N_EX

EX = ("z", "xh")
PLANE = ("xl", "y")
FEAT = ("xl", "y", "c")

LANES = (((1,), (1,)), ((), ()))


def dot_t(a, b, precision=HIGH):
    return lax.dot_general(a, b, LANES, precision=precision, preferred_element_type=F32)


def iota(shape, dim):
    return lax.broadcasted_iota(jnp.int32, shape, dim)


def to_row(col, offset=0):
    n = col.shape[0]
    place = iota((n, 128), 1) == iota((n, 128), 0) + offset
    return jnp.sum(jnp.where(place, col, 0.0), axis=0, keepdims=True)


def to_col(row, n, offset=0):
    place = iota((n, 128), 1) == iota((n, 128), 0) + offset
    return jnp.sum(jnp.where(place, row, 0.0), axis=1, keepdims=True)


def call(kernel, outs, *args, smem=0, hbm=0, space=pltpu.VMEM, scratch=()):
    vmem = len(args) - smem - hbm
    spaces = [pltpu.SMEM] * smem + [pltpu.VMEM] * vmem + [pl.ANY] * hbm
    args = list(args)
    for i in range(smem, smem + vmem):
        args[i] = pltpu.with_memory_space_constraint(args[i], pltpu.VMEM)
    for i in range(smem + vmem, len(args)):
        args[i] = pltpu.with_memory_space_constraint(args[i], pltpu.HBM)
    many = isinstance(outs, list)
    out_spec = pl.BlockSpec(memory_space=pltpu.VMEM)
    return pl.pallas_call(
        kernel,
        out_shape=[space(s, d) for s, d in outs] if many else space(*outs),
        in_specs=[pl.BlockSpec(memory_space=m) for m in spaces],
        out_specs=[out_spec] * len(outs) if many else out_spec,
        scratch_shapes=scratch,
        compiler_params=pltpu.CompilerParams(vmem_limit_bytes=12 << 20),
    )(*args)


def pick_kernel(spot_ref, index_ref, ft_hbm, out_ref, both_ref, sem):
    both_ref[...] = jnp.zeros_like(both_ref)
    low = pltpu.make_async_copy(ft_hbm, both_ref.at[0:SLICE, 0:ROWS], sem.at[0])
    high = pltpu.make_async_copy(ft_hbm, both_ref.at[SLICE : 2 * SLICE, ROWS : 2 * ROWS], sem.at[1])
    low.start()
    high.start()
    core, base = spot_ref[3], spot_ref[4]
    lane = iota((OWN, ROWS), 1)
    index = index_ref[...]
    blocks = iota((OWN, N_FEAT), 1)

    def mask(block):
        col = jnp.sum(jnp.where(blocks == block, index, 0), axis=1, keepdims=True) - base
        return (lane == col).astype(F32).astype(BF16)

    def masks(side):
        return jnp.concatenate([mask(2 * p + side) for p in range(N_PLANE)], axis=0)

    chosen = jnp.concatenate([masks(core), masks(1 - core)], axis=1)
    low.wait()
    high.wait()
    both = lax.dot_general(chosen, both_ref[...], LANES, preferred_element_type=F32)
    out_ref[...] = both.astype(BF16).reshape(N_PLANE, OWN, 2 * SLICE)


def spread_kernel(spot_ref, in_ref, out_ref):
    low = iota((OWN, 128), 1) < SLICE
    side, y = spot_ref[0], spot_ref[1]
    for t, offset in enumerate(OFFSETS):
        row = lax.rem(y + (offset + N_Y), N_Y)
        a = in_ref[side * N_Y + row].astype(F32)
        b = in_ref[(1 - side) * N_Y + row].astype(F32)
        own = jnp.where(low, a, pltpu.roll(b, SLICE, 1)).astype(BF16)
        other = jnp.where(low, pltpu.roll(a, SLICE, 1), b).astype(BF16)
        cols = slice(128 * t, 128 * t + 128)
        for i in range(N_EX):
            out_ref[i, 0:OWN, cols] = own
            out_ref[i, OWN : 2 * OWN, cols] = other


def diagonal():
    return iota((BLOCK, BLOCK), 0) == iota((BLOCK, BLOCK), 1)


def half_dots(ft, cen_ref, first):
    block = cen_ref[:, first : first + OWN, :].reshape(BLOCK, WIDTH)
    squares = jnp.sum(jnp.square(block.astype(F32)), axis=1, keepdims=True)
    squares = jnp.sum(jnp.where(diagonal(), squares, 0.0), axis=0, keepdims=True)
    return jnp.dot(block, ft, preferred_element_type=F32), squares


def load_features(chunk_hbm, near_ref, far_ref, ft_ref, sems):
    copies = []
    for i, chunk in enumerate(chunk_hbm):
        copies.append(pltpu.make_async_copy(chunk, ft_ref.at[128 * i : 128 * i + 128], sems.at[i]))
        copies[-1].start()
    first = 128 * len(chunk_hbm)
    ft_ref[first : first + SLICE] = near_ref[...]
    ft_ref[first + SLICE : first + 2 * SLICE] = far_ref[...]
    return copies


def other_kernel(near_ref, far_ref, cen_ref, *refs):
    *chunk_hbm, out_ref, ft_ref, sems = refs
    copies = load_features(chunk_hbm, near_ref, far_ref, ft_ref, sems)

    def squares(start):
        return jnp.sum(jnp.square(ft_ref[start : start + 128].astype(F32)), axis=0, keepdims=True)

    row_sq = squares(128 * len(chunk_hbm))
    for i, copy in enumerate(copies):
        copy.wait()
        row_sq += squares(128 * i)
    out_ref[BLOCK : BLOCK + 8, :] = jnp.zeros((8, ROWS), F32)
    out_ref[BLOCK : BLOCK + 1, :] = row_sq
    dots, squares = half_dots(ft_ref[...], cen_ref, OWN)
    out_ref[0:BLOCK, :] = dots
    out_ref[BLOCK + 1 : BLOCK + 2, 0:BLOCK] = squares


def own_kernel(near_ref, far_ref, cen_ref, *refs):
    *chunk_hbm, dots_ref, squares_ref, ft_ref, sems = refs
    for copy in load_features(chunk_hbm, near_ref, far_ref, ft_ref, sems):
        copy.wait()
    dots, squares = half_dots(ft_ref[...], cen_ref, 0)
    dots_ref[...] = dots
    squares_ref[...] = jnp.broadcast_to(squares, (8, BLOCK))


def split2(x):
    high = x.astype(BF16)
    return high, (x - high.astype(F32)).astype(BF16)


def split3(x):
    high = x.astype(BF16).astype(F32)
    rest = x - high
    mid = rest.astype(BF16).astype(F32)
    return jnp.concatenate([high, mid, rest - mid], axis=0).astype(BF16)


def fold3(y):
    n = y.shape[0] // 3
    return y[0:n] + (y[n : 2 * n] + y[2 * n : 3 * n])


def panel_kernel(
    dots_ref, squares_ref, sent_ref, labels_ref, loc_ref, recv_hbm, high_ref, low_ref, place_ref, out_ref, recv_ref, sem
):
    copy = pltpu.make_async_copy(recv_hbm, recv_ref, sem)
    copy.start()
    place_ref[...] = (iota((BLOCK, ROWS), 1) == loc_ref[...]).astype(F32).astype(BF16)
    hit = iota((CLASSES, ROWS), 0) == labels_ref[...]
    targets = jnp.where(hit, CLASSES - 1.0, -1.0).astype(BF16)
    copy.wait()
    row_sq = sent_ref[BLOCK : BLOCK + 1, :] + recv_ref[BLOCK : BLOCK + 1, :]
    centre_sq = squares_ref[0:1, :] + recv_ref[BLOCK + 1 : BLOCK + 2, 0:BLOCK]
    centre_sq = jnp.sum(jnp.where(diagonal(), centre_sq, 0.0), axis=1, keepdims=True)
    row_scale = lax.rsqrt(row_sq / F + EPS)
    centre_scale = lax.rsqrt(centre_sq / F + EPS)
    dots = dots_ref[...] + recv_ref[0:BLOCK, :]
    cosine = jnp.clip(dots * row_scale * centre_scale, -1.0, 1.0)
    high, low = split2(jnp.exp(GAMMA * (cosine - 1.0)))
    high_ref[...] = high
    low_ref[...] = low
    rhs = (dot_t(targets, high, None) + dot_t(targets, low, None)) / EXAMPLES
    for i in range(N_EX):
        out_ref[i] = rhs


def apply_panel(vec, high_ref, low_ref, place_ref):
    parts = split3(vec)

    def times(matrix):
        return fold3(jnp.dot(parts, matrix, preferred_element_type=F32))

    k = times(high_ref[...]) + times(low_ref[...])
    return k, k / EXAMPLES + LAMBDA * times(place_ref[...])


def apply_normal(k, high_ref, low_ref, place_ref):
    parts = split3(k)

    def times(matrix):
        return fold3(dot_t(parts, matrix, None))

    return (times(high_ref[...]) + times(low_ref[...])) / EXAMPLES + LAMBDA * times(place_ref[...])


def total(ref):
    acc = ref[0]
    for i in range(1, ref.shape[0]):
        acc = acc + ref[i]
    return acc


def put_chunks(out_ref, vec, stride, slot):
    for s in range(N_FEAT):
        g, l = s // 8, s % 8
        out_ref[s * stride + slot] = vec[4 * g : 4 * g + 4, 128 * l : 128 * l + 128]


def take_chunks(in_ref, stride, out_ref):
    for s in range(N_FEAT):
        g, l = s // 8, s % 8
        out_ref[4 * g : 4 * g + 4, 128 * l : 128 * l + 128] = in_ref[s * stride]


def sum_slot(ref, stride, slot):
    acc = ref[slot]
    for s in range(1, N_FEAT):
        acc = acc + ref[s * stride + slot]
    return acc


def first_kernel(recv_ref, pre_ref, high_ref, low_ref, place_ref, rhs_ref, u_ref, out_ref):
    rhs = total(recv_ref)
    u = dot_t(rhs, pre_ref[...])
    rhs_ref[...] = rhs
    u_ref[...] = u
    k, g = apply_panel(u, high_ref, low_ref, place_ref)
    put_chunks(out_ref, k, 2, 0)
    put_chunks(out_ref, g, 2, 1)


def chunk_kernel(recv_ref, chunk_ref, out_ref):
    k = sum_slot(recv_ref, 2, 0)
    chunk_ref[0] = k
    chunk_ref[1] = sum_slot(recv_ref, 2, 1)
    for s in range(N_FEAT):
        out_ref[s] = k


def normal_kernel(recv_ref, high_ref, low_ref, place_ref, k_ref, out_ref):
    take_chunks(recv_ref, 1, k_ref)
    image = apply_normal(k_ref[...], high_ref, low_ref, place_ref)
    for i in range(N_EX):
        out_ref[i] = image


def second_kernel(recv_ref, pre_ref, high_ref, low_ref, place_ref, rhs_ref, u_ref, image_ref, v_ref, out_ref):
    image = total(recv_ref)
    v = dot_t(image, pre_ref[...])
    image_ref[...] = image
    v_ref[...] = v
    k, g = apply_panel(v, high_ref, low_ref, place_ref)
    put_chunks(out_ref, k, 3, 0)
    put_chunks(out_ref, g, 3, 1)
    u = u_ref[...]
    row = to_row(jnp.sum(rhs_ref[...] * u, axis=1, keepdims=True), 0)
    row = row + to_row(jnp.sum(u * image, axis=1, keepdims=True), CLASSES)
    row = row + to_row(jnp.sum(v * image, axis=1, keepdims=True), 2 * CLASSES)
    row = jnp.broadcast_to(row, (4, 128))
    for s in range(N_FEAT):
        out_ref[s * 3 + 2] = row


def step_kernel(spot_ref, recv_ref, chunk_ref, rhs_ref, u_ref, image_ref, v_ref, scal_ref, out_ref):
    row = sum_slot(recv_ref, 3, 2)[0:1]
    scal_ref[...] = jnp.broadcast_to(row, (8, 128))
    alpha = to_col(row, CLASSES, 0) / to_col(row, CLASSES, CLASSES)
    residual = rhs_ref[...] - alpha * image_ref[...]
    z = u_ref[...] - alpha * v_ref[...]
    rz = to_row(jnp.sum(residual * z, axis=1, keepdims=True))
    alpha_row = to_row(alpha)
    first = spot_ref[2] * 4
    mine = iota((4, 128), 1) == iota((4, 128), 0) + first
    alpha_mine = jnp.sum(jnp.where(mine, alpha_row, 0.0), axis=1, keepdims=True)
    kz = chunk_ref[0] - alpha_mine * sum_slot(recv_ref, 3, 0)
    gz = chunk_ref[1] - alpha_mine * sum_slot(recv_ref, 3, 1)
    quad = jnp.sum(kz * gz, axis=1, keepdims=True)
    quad_row = jnp.sum(jnp.where(mine, quad, 0.0), axis=0, keepdims=True)
    which = iota((4, 128), 0)
    tail = jnp.where(which == 0, rz, jnp.where(which == 1, quad_row, 0.0))
    for s in range(N_FEAT):
        out_ref[s * 2] = kz
        out_ref[s * 2 + 1] = tail


def gather_kernel(recv_ref, kz_ref, tail_ref, out_ref):
    take_chunks(recv_ref, 2, kz_ref)
    tail = sum_slot(recv_ref, 2, 1)
    tail_ref[...] = tail
    for i in range(N_EX):
        out_ref[i] = tail[1:2]


def last_kernel(recv_ref, tail_ref, scal_ref, k_ref, kz_ref, out_ref):
    quad = to_col(total(recv_ref), CLASSES)
    rz_next = to_col(tail_ref[0:1, :], CLASSES)
    row = scal_ref[0:1, :]
    rz = to_col(row, CLASSES, 0)
    uu = to_col(row, CLASSES, CLASSES)
    vu = to_col(row, CLASSES, 2 * CLASSES)
    alpha = rz / uu
    beta = rz_next / rz
    cross = uu - alpha * vu
    alpha_next = rz_next / (quad + 2.0 * beta * cross + beta * beta * uu)
    k = k_ref[...]
    out_ref[...] = alpha * k + alpha_next * (kz_ref[...] + beta * k)


def predict(features, centre_index, labels, precond):
    ex_index = lax.axis_index(EX)
    feat_index = lax.axis_index(FEAT)
    core = lax.axis_index("c")
    local = centre_index[:, 0, :] - ex_index * ROWS
    ft_local = features.T
    swapped = lax.ppermute(ft_local, "xl", [(0, 1), (1, 0)])
    here = jnp.concatenate([ft_local, swapped], axis=0)
    up = [(i, (i + 1) % N_Y) for i in range(N_Y)]
    down = [(i, (i - 1) % N_Y) for i in range(N_Y)]
    chunks = [here]
    below = above = here
    for _ in range(3):
        below = lax.ppermute(below, "y", up)
        above = lax.ppermute(above, "y", down)
        chunks += [below, above]
    chunks += [lax.ppermute(below[:SLICE], "y", up), lax.ppermute(above[SLICE:], "y", down)]

    spot = jnp.stack([lax.axis_index("xl"), lax.axis_index("y"), feat_index // 8, core, ex_index * ROWS])
    picked = call(
        pick_kernel, ((N_PLANE, OWN, 2 * SLICE), BF16), spot, centre_index[:, 0, :].T, ft_local, smem=1, hbm=1,
        scratch=[pltpu.VMEM((2 * SLICE, 2 * ROWS), BF16), pltpu.SemaphoreType.DMA((2,))],
    )
    picked = lax.all_to_all(picked, PLANE, 0, 0, tiled=True)
    spread = call(spread_kernel, ((N_EX, 2 * OWN, WIDTH), BF16), spot, picked, smem=1)
    cen = lax.all_to_all(spread, EX, 0, 0, tiled=True)

    own_rows = lax.dynamic_index_in_dim(local, feat_index, 0, keepdims=False)
    slot = lax.iota(jnp.int32, N_EX)[:, None] == ex_index
    loc = jnp.where(slot, own_rows[None, :], -1).reshape(BLOCK, 1)

    dots_t = ((BLOCK, ROWS), F32)
    operands = (*chunks[-2:], cen, *chunks[:-2])
    still = len(chunks) - 2
    scratch = [pltpu.VMEM((WIDTH, ROWS), BF16), pltpu.SemaphoreType.DMA((still,))]
    sent = call(other_kernel, ((BLOCK + 8, ROWS), F32), *operands, hbm=still, scratch=scratch)
    got = lax.ppermute(sent, "c", [(0, 1), (1, 0)])
    own, own_sq = call(own_kernel, [dots_t, ((8, BLOCK), F32)], *operands, hbm=still, scratch=scratch)
    half_t = ((BLOCK, ROWS), BF16)
    high, low, place, part = call(
        panel_kernel, [half_t, half_t, half_t, ((N_EX, CLASSES, BLOCK), F32)],
        own, own_sq, sent, labels.reshape(1, ROWS), loc, got, hbm=1,
        scratch=[pltpu.VMEM(sent.shape, F32), pltpu.SemaphoreType.DMA],
    )
    vec = ((CLASSES, BLOCK), F32)
    part = lax.all_to_all(part, EX, 0, 0, tiled=True)
    rhs, u, part = call(first_kernel, [vec, vec, ((N_FEAT * 2, 4, 128), F32)], part, precond, high, low, place)
    part = lax.all_to_all(part, FEAT, 0, 0, tiled=True)
    chunk, part = call(chunk_kernel, [((2, 4, 128), F32), ((N_FEAT, 4, 128), F32)], part)
    part = lax.all_to_all(part, FEAT, 0, 0, tiled=True)
    k, part = call(normal_kernel, [((CLASSES, ROWS), F32), ((N_EX, CLASSES, BLOCK), F32)], part, high, low, place)
    part = lax.all_to_all(part, EX, 0, 0, tiled=True)
    image, v, part = call(
        second_kernel, [vec, vec, ((N_FEAT * 3, 4, 128), F32)],
        part, precond, high, low, place, rhs, u,
    )
    part = lax.all_to_all(part, FEAT, 0, 0, tiled=True)
    scal, part = call(
        step_kernel, [((8, 128), F32), ((N_FEAT * 2, 4, 128), F32)],
        spot, part, chunk, rhs, u, image, v, smem=1,
    )
    part = lax.all_to_all(part, FEAT, 0, 0, tiled=True)
    kz, tail, part = call(gather_kernel, [((CLASSES, ROWS), F32), ((4, 128), F32), ((N_EX, 1, 128), F32)], part)
    part = lax.all_to_all(part, EX, 0, 0, tiled=True)
    out = call(last_kernel, ((CLASSES, ROWS), F32), part, tail, scal, k, kz, space=jax.ShapeDtypeStruct)
    return out.T


def solution(mesh):
    fine = Mesh(mesh.devices.reshape(8, 2, 2, 8, 2), ("z", "xh", "xl", "y", "c"))
    in_specs = (P(EX, FEAT), P(None, EX, None), P(EX), P(FEAT, None))
    return jax.shard_map(predict, mesh=fine, in_specs=in_specs, out_specs=P(EX, None), check_vma=False)
```

```python
import jax
import jax.numpy as jnp
from jax import lax
from jax.experimental import pallas as pl
from jax.experimental.pallas import tpu as pltpu
from jax.sharding import Mesh, PartitionSpec as P


CLASSES = 16
GAMMA = 4.0
LAMBDA = 0.05
EPS = 1e-06
HIGH = lax.Precision.HIGHEST
F32 = jnp.float32
BF16 = jnp.bfloat16

ROWS = 1024
BLOCK = 256
OWN = 16
N_EX = 16
N_FEAT = 32
N_PLANE = 16
SLICE = 64
WIDTH = N_PLANE * SLICE
F = 2048
N_Y = 8
OFFSETS = (0, -1, 1, -2, 2, -3, 3, 4)
EXAMPLES = ROWS * N_EX

EX = ("z", "xh")
PLANE = ("xl", "y")
FEAT = ("xl", "y", "c")

LANES = (((1,), (1,)), ((), ()))


def dot_t(a, b, precision=HIGH):
    return lax.dot_general(a, b, LANES, precision=precision, preferred_element_type=F32)


def iota(shape, dim):
    return lax.broadcasted_iota(jnp.int32, shape, dim)


def to_row(col, offset=0):
    n = col.shape[0]
    place = iota((n, 128), 1) == iota((n, 128), 0) + offset
    return jnp.sum(jnp.where(place, col, 0.0), axis=0, keepdims=True)


def to_col(row, n, offset=0):
    place = iota((n, 128), 1) == iota((n, 128), 0) + offset
    return jnp.sum(jnp.where(place, row, 0.0), axis=1, keepdims=True)


def call(kernel, outs, *args, smem=0, hbm=0, space=pltpu.VMEM, scratch=()):
    vmem = len(args) - smem - hbm
    spaces = [pltpu.SMEM] * smem + [pltpu.VMEM] * vmem + [pl.ANY] * hbm
    args = list(args)
    for i in range(smem, smem + vmem):
        args[i] = pltpu.with_memory_space_constraint(args[i], pltpu.VMEM)
    for i in range(smem + vmem, len(args)):
        args[i] = pltpu.with_memory_space_constraint(args[i], pltpu.HBM)
    many = isinstance(outs, list)
    out_spec = pl.BlockSpec(memory_space=pltpu.VMEM)
    return pl.pallas_call(
        kernel,
        out_shape=[space(s, d) for s, d in outs] if many else space(*outs),
        in_specs=[pl.BlockSpec(memory_space=m) for m in spaces],
        out_specs=[out_spec] * len(outs) if many else out_spec,
        scratch_shapes=scratch,
        compiler_params=pltpu.CompilerParams(vmem_limit_bytes=12 << 20),
    )(*args)


def pick_kernel(spot_ref, index_ref, ft_hbm, out_ref, mine_ref, ft_ref, sem):
    copy = pltpu.make_async_copy(ft_hbm, ft_ref, sem)
    copy.start()
    core, base = spot_ref[3], spot_ref[4]
    mine_ref[...] = (iota((4, 128), 1) == iota((4, 128), 0) + spot_ref[2] * 4).astype(F32)
    lane = iota((OWN, ROWS), 1)
    index = index_ref[...]
    blocks = iota((OWN, N_FEAT), 1)

    def mask(block):
        col = jnp.sum(jnp.where(blocks == block, index, 0), axis=1, keepdims=True) - base
        return (lane == col).astype(F32).astype(BF16)

    def chosen(side, table):
        masks = jnp.concatenate([mask(2 * p + side) for p in range(N_PLANE)], axis=0)
        return lax.dot_general(masks, table, LANES, preferred_element_type=F32)

    copy.wait()
    ft = ft_ref[...]
    zero = jnp.zeros_like(ft)
    both = chosen(core, jnp.concatenate([ft, zero], axis=0)) + chosen(1 - core, jnp.concatenate([zero, ft], axis=0))
    out_ref[...] = both.astype(BF16).reshape(N_PLANE, OWN, 2 * SLICE)


def spread_kernel(spot_ref, in_ref, out_ref):
    low = iota((OWN, 128), 1) < SLICE
    side, y = spot_ref[0], spot_ref[1]
    sign = 1 - 2 * spot_ref[3]
    for t, offset in enumerate(OFFSETS):
        row = lax.rem(y + N_Y + sign * offset, N_Y)
        a = in_ref[side * N_Y + row].astype(F32)
        b = in_ref[(1 - side) * N_Y + row].astype(F32)
        own = jnp.where(low, a, pltpu.roll(b, SLICE, 1)).astype(BF16)
        other = jnp.where(low, pltpu.roll(a, SLICE, 1), b).astype(BF16)
        cols = slice(128 * t, 128 * t + 128)
        for i in range(N_EX):
            out_ref[i, 0:OWN, cols] = own
            out_ref[i, OWN : 2 * OWN, cols] = other


def diagonal():
    return iota((BLOCK, BLOCK), 0) == iota((BLOCK, BLOCK), 1)


def half_dots(ft, cen_ref, first):
    block = cen_ref[:, first : first + OWN, :].reshape(BLOCK, WIDTH)
    squares = jnp.sum(jnp.square(block.astype(F32)), axis=1, keepdims=True)
    squares = jnp.sum(jnp.where(diagonal(), squares, 0.0), axis=0, keepdims=True)
    return jnp.dot(block, ft, preferred_element_type=F32), squares


def load_features(chunk_hbm, near_ref, far_ref, ft_ref, sems):
    copies = []
    for i, chunk in enumerate(chunk_hbm):
        copies.append(pltpu.make_async_copy(chunk, ft_ref.at[128 * i : 128 * i + 128], sems.at[i]))
        copies[-1].start()
    first = 128 * len(chunk_hbm)
    ft_ref[first : first + SLICE] = near_ref[...]
    ft_ref[first + SLICE : first + 2 * SLICE] = far_ref[...]
    return copies


def other_kernel(near_ref, far_ref, cen_ref, *refs):
    *chunk_hbm, out_ref, ft_ref, sems = refs
    copies = load_features(chunk_hbm, near_ref, far_ref, ft_ref, sems)

    def squares(start):
        return jnp.sum(jnp.square(ft_ref[start : start + 128].astype(F32)), axis=0, keepdims=True)

    row_sq = squares(128 * len(chunk_hbm))
    for i, copy in enumerate(copies):
        copy.wait()
        row_sq += squares(128 * i)
    out_ref[BLOCK : BLOCK + 8, :] = jnp.zeros((8, ROWS), F32)
    out_ref[BLOCK : BLOCK + 1, :] = row_sq
    dots, squares = half_dots(ft_ref[...], cen_ref, OWN)
    out_ref[0:BLOCK, :] = dots
    out_ref[BLOCK + 1 : BLOCK + 2, 0:BLOCK] = squares


def own_kernel(near_ref, far_ref, cen_ref, *refs):
    *chunk_hbm, dots_ref, squares_ref, ft_ref, sems = refs
    for copy in load_features(chunk_hbm, near_ref, far_ref, ft_ref, sems):
        copy.wait()
    dots, squares = half_dots(ft_ref[...], cen_ref, 0)
    dots_ref[...] = dots
    squares_ref[...] = jnp.broadcast_to(squares, (8, BLOCK))


def split2(x):
    high = x.astype(BF16)
    return high, (x - high.astype(F32)).astype(BF16)


def split3(x):
    high = x.astype(BF16).astype(F32)
    rest = x - high
    mid = rest.astype(BF16).astype(F32)
    return jnp.concatenate([high, mid, rest - mid], axis=0).astype(BF16)


def fold3(y):
    n = y.shape[0] // 3
    return y[0:n] + (y[n : 2 * n] + y[2 * n : 3 * n])


def panel_kernel(
    dots_ref, squares_ref, sent_ref, labels_ref, loc_ref, recv_hbm, high_ref, low_ref, place_ref, out_ref, recv_ref, sem
):
    copy = pltpu.make_async_copy(recv_hbm, recv_ref, sem)
    copy.start()
    place_ref[...] = (iota((BLOCK, ROWS), 1) == loc_ref[...]).astype(F32).astype(BF16)
    hit = iota((CLASSES, ROWS), 0) == labels_ref[...]
    targets = jnp.where(hit, CLASSES - 1.0, -1.0).astype(BF16)
    copy.wait()
    row_sq = sent_ref[BLOCK : BLOCK + 1, :] + recv_ref[BLOCK : BLOCK + 1, :]
    centre_sq = squares_ref[0:1, :] + recv_ref[BLOCK + 1 : BLOCK + 2, 0:BLOCK]
    centre_sq = jnp.sum(jnp.where(diagonal(), centre_sq, 0.0), axis=1, keepdims=True)
    row_scale = lax.rsqrt(row_sq / F + EPS)
    centre_scale = lax.rsqrt(centre_sq / F + EPS)
    dots = dots_ref[...] + recv_ref[0:BLOCK, :]
    cosine = jnp.clip(dots * row_scale * centre_scale, -1.0, 1.0)
    high, low = split2(jnp.exp(GAMMA * (cosine - 1.0)))
    high_ref[...] = high
    low_ref[...] = low
    rhs = (dot_t(targets, high, None) + dot_t(targets, low, None)) / EXAMPLES
    for i in range(N_EX):
        out_ref[i] = rhs


def apply_panel(vec, high_ref, low_ref, place_ref):
    parts = split3(vec)

    def times(matrix):
        return fold3(jnp.dot(parts, matrix, preferred_element_type=F32))

    k = times(high_ref[...]) + times(low_ref[...])
    return k, k / EXAMPLES + LAMBDA * times(place_ref[...])


def apply_normal(k, high_ref, low_ref, place_ref):
    parts = split3(k)

    def times(matrix):
        return fold3(dot_t(parts, matrix, None))

    return (times(high_ref[...]) + times(low_ref[...])) / EXAMPLES + LAMBDA * times(place_ref[...])


def total(ref):
    acc = ref[0]
    for i in range(1, ref.shape[0]):
        acc = acc + ref[i]
    return acc


def put_chunks(out_ref, vec, stride, slot):
    for s in range(N_FEAT):
        g, l = s // 8, s % 8
        out_ref[s * stride + slot] = vec[4 * g : 4 * g + 4, 128 * l : 128 * l + 128]


def take_chunks(in_ref, stride, out_ref):
    for s in range(N_FEAT):
        g, l = s // 8, s % 8
        out_ref[4 * g : 4 * g + 4, 128 * l : 128 * l + 128] = in_ref[s * stride]


def sum_slot(ref, stride, slot):
    acc = ref[slot]
    for s in range(1, N_FEAT):
        acc = acc + ref[s * stride + slot]
    return acc


def first_kernel(recv_ref, pre_ref, high_ref, low_ref, place_ref, rhs_ref, u_ref, out_ref):
    rhs = total(recv_ref)
    u = dot_t(rhs, pre_ref[...])
    rhs_ref[...] = rhs
    u_ref[...] = u
    k, g = apply_panel(u, high_ref, low_ref, place_ref)
    put_chunks(out_ref, k, 2, 0)
    put_chunks(out_ref, g, 2, 1)


def chunk_kernel(recv_ref, chunk_ref, out_ref):
    k = sum_slot(recv_ref, 2, 0)
    chunk_ref[0] = k
    chunk_ref[1] = sum_slot(recv_ref, 2, 1)
    for s in range(N_FEAT):
        out_ref[s] = k


def normal_kernel(recv_ref, high_ref, low_ref, place_ref, k_ref, out_ref):
    take_chunks(recv_ref, 1, k_ref)
    image = apply_normal(k_ref[...], high_ref, low_ref, place_ref)
    for i in range(N_EX):
        out_ref[i] = image


def second_kernel(recv_ref, pre_ref, high_ref, low_ref, place_ref, rhs_ref, u_ref, image_ref, v_ref, out_ref):
    image = total(recv_ref)
    v = dot_t(image, pre_ref[...])
    image_ref[...] = image
    v_ref[...] = v
    k, g = apply_panel(v, high_ref, low_ref, place_ref)
    put_chunks(out_ref, k, 3, 0)
    put_chunks(out_ref, g, 3, 1)
    u = u_ref[...]
    row = to_row(jnp.sum(rhs_ref[...] * u, axis=1, keepdims=True), 0)
    row = row + to_row(jnp.sum(u * image, axis=1, keepdims=True), CLASSES)
    row = row + to_row(jnp.sum(v * image, axis=1, keepdims=True), 2 * CLASSES)
    row = jnp.broadcast_to(row, (4, 128))
    for s in range(N_FEAT):
        out_ref[s * 3 + 2] = row


def step_kernel(mine_ref, recv_ref, chunk_ref, rhs_ref, u_ref, image_ref, v_ref, scal_ref, out_ref):
    row = sum_slot(recv_ref, 3, 2)[0:1]
    scal_ref[...] = jnp.broadcast_to(row, (8, 128))
    alpha = to_col(row, CLASSES, 0) / to_col(row, CLASSES, CLASSES)
    residual = rhs_ref[...] - alpha * image_ref[...]
    z = u_ref[...] - alpha * v_ref[...]
    rz = to_row(jnp.sum(residual * z, axis=1, keepdims=True))
    alpha_row = to_row(alpha)
    mine = mine_ref[...]
    alpha_mine = jnp.sum(mine * alpha_row, axis=1, keepdims=True)
    kz = chunk_ref[0] - alpha_mine * sum_slot(recv_ref, 3, 0)
    gz = chunk_ref[1] - alpha_mine * sum_slot(recv_ref, 3, 1)
    quad = jnp.sum(kz * gz, axis=1, keepdims=True)
    quad_row = jnp.sum(mine * quad, axis=0, keepdims=True)
    which = iota((4, 128), 0)
    tail = jnp.where(which == 0, rz, jnp.where(which == 1, quad_row, 0.0))
    for s in range(N_FEAT):
        out_ref[s * 2] = kz
        out_ref[s * 2 + 1] = tail


def gather_kernel(recv_ref, kz_ref, tail_ref, out_ref):
    take_chunks(recv_ref, 2, kz_ref)
    tail = sum_slot(recv_ref, 2, 1)
    tail_ref[...] = tail
    for i in range(N_EX):
        out_ref[i] = tail[1:2]


def last_kernel(recv_ref, tail_ref, scal_ref, k_ref, kz_ref, out_ref):
    quad = to_col(total(recv_ref), CLASSES)
    rz_next = to_col(tail_ref[0:1, :], CLASSES)
    row = scal_ref[0:1, :]
    rz = to_col(row, CLASSES, 0)
    uu = to_col(row, CLASSES, CLASSES)
    vu = to_col(row, CLASSES, 2 * CLASSES)
    alpha = rz / uu
    beta = rz_next / rz
    cross = uu - alpha * vu
    alpha_next = rz_next / (quad + 2.0 * beta * cross + beta * beta * uu)
    k = k_ref[...]
    out_ref[...] = alpha * k + alpha_next * (kz_ref[...] + beta * k)


def predict(features, centre_index, labels, precond):
    ex_index = lax.axis_index(EX)
    feat_index = lax.axis_index(FEAT)
    core = lax.axis_index("c")
    local = centre_index[:, 0, :] - ex_index * ROWS
    ft_local = features.T
    swapped = lax.ppermute(ft_local, "xl", [(0, 1), (1, 0)])
    here = jnp.concatenate([ft_local, swapped], axis=0)
    up = [(2 * i + c, 2 * ((i + 1 - 2 * c) % N_Y) + c) for i in range(N_Y) for c in range(2)]
    down = [(2 * i + c, 2 * ((i - 1 + 2 * c) % N_Y) + c) for i in range(N_Y) for c in range(2)]
    chunks = [here]
    below = above = here
    for _ in range(3):
        below = lax.ppermute(below, ("y", "c"), up)
        above = lax.ppermute(above, ("y", "c"), down)
        chunks += [below, above]
    chunks += [lax.ppermute(below[:SLICE], ("y", "c"), up), lax.ppermute(above[SLICE:], ("y", "c"), down)]

    spot = jnp.stack([lax.axis_index("xl"), lax.axis_index("y"), feat_index // 8, core, ex_index * ROWS])
    picked, mine = call(
        pick_kernel, [((N_PLANE, OWN, 2 * SLICE), BF16), ((4, 128), F32)], spot, centre_index[:, 0, :].T, ft_local, smem=1, hbm=1,
        scratch=[pltpu.VMEM((SLICE, ROWS), BF16), pltpu.SemaphoreType.DMA],
    )
    picked = lax.all_to_all(picked, PLANE, 0, 0, tiled=True)
    spread = call(spread_kernel, ((N_EX, 2 * OWN, WIDTH), BF16), spot, picked, smem=1)
    cen = lax.all_to_all(spread, EX, 0, 0, tiled=True)

    own_rows = lax.dynamic_index_in_dim(local, feat_index, 0, keepdims=False)
    slot = lax.iota(jnp.int32, N_EX)[:, None] == ex_index
    loc = jnp.where(slot, own_rows[None, :], -1).reshape(BLOCK, 1)

    dots_t = ((BLOCK, ROWS), F32)
    operands = (*chunks[-2:], cen, *chunks[:-2])
    still = len(chunks) - 2
    scratch = [pltpu.VMEM((WIDTH, ROWS), BF16), pltpu.SemaphoreType.DMA((still,))]
    sent = call(other_kernel, ((BLOCK + 8, ROWS), F32), *operands, hbm=still, scratch=scratch)
    got = lax.ppermute(sent, "c", [(0, 1), (1, 0)])
    own, own_sq = call(own_kernel, [dots_t, ((8, BLOCK), F32)], *operands, hbm=still, scratch=scratch)
    half_t = ((BLOCK, ROWS), BF16)
    high, low, place, part = call(
        panel_kernel, [half_t, half_t, half_t, ((N_EX, CLASSES, BLOCK), F32)],
        own, own_sq, sent, labels.reshape(1, ROWS), loc, got, hbm=1,
        scratch=[pltpu.VMEM(sent.shape, F32), pltpu.SemaphoreType.DMA],
    )
    vec = ((CLASSES, BLOCK), F32)
    part = lax.all_to_all(part, EX, 0, 0, tiled=True)
    rhs, u, part = call(first_kernel, [vec, vec, ((N_FEAT * 2, 4, 128), F32)], part, precond, high, low, place)
    part = lax.all_to_all(part, FEAT, 0, 0, tiled=True)
    chunk, part = call(chunk_kernel, [((2, 4, 128), F32), ((N_FEAT, 4, 128), F32)], part)
    part = lax.all_to_all(part, FEAT, 0, 0, tiled=True)
    k, part = call(normal_kernel, [((CLASSES, ROWS), F32), ((N_EX, CLASSES, BLOCK), F32)], part, high, low, place)
    part = lax.all_to_all(part, EX, 0, 0, tiled=True)
    image, v, part = call(
        second_kernel, [vec, vec, ((N_FEAT * 3, 4, 128), F32)],
        part, precond, high, low, place, rhs, u,
    )
    part = lax.all_to_all(part, FEAT, 0, 0, tiled=True)
    scal, part = call(
        step_kernel, [((8, 128), F32), ((N_FEAT * 2, 4, 128), F32)],
        mine, part, chunk, rhs, u, image, v,
    )
    part = lax.all_to_all(part, FEAT, 0, 0, tiled=True)
    kz, tail, part = call(gather_kernel, [((CLASSES, ROWS), F32), ((4, 128), F32), ((N_EX, 1, 128), F32)], part)
    part = lax.all_to_all(part, EX, 0, 0, tiled=True)
    out = call(last_kernel, ((CLASSES, ROWS), F32), part, tail, scal, k, kz, space=jax.ShapeDtypeStruct)
    return out.T


def solution(mesh):
    fine = Mesh(mesh.devices.reshape(8, 2, 2, 8, 2), ("z", "xh", "xl", "y", "c"))
    in_specs = (P(EX, FEAT), P(None, EX, None), P(EX), P(FEAT, None))
    return jax.shard_map(predict, mesh=fine, in_specs=in_specs, out_specs=P(EX, None), check_vma=False)
```

```python
import jax
import jax.numpy as jnp
from jax import lax
from jax.experimental import pallas as pl
from jax.experimental.pallas import tpu as pltpu
from jax.sharding import Mesh, PartitionSpec as P


CLASSES = 16
GAMMA = 4.0
LAMBDA = 0.05
EPS = 1e-06
HIGH = lax.Precision.HIGHEST
F32 = jnp.float32
BF16 = jnp.bfloat16

ROWS = 1024
BLOCK = 256
OWN = 16
N_EX = 16
N_FEAT = 32
N_PLANE = 16
SLICE = 64
WIDTH = N_PLANE * SLICE
F = 2048
N_Y = 8
OFFSETS = (0, -1, 1, -2, 2, -3, 3, -4)
EXAMPLES = ROWS * N_EX

EX = ("z", "xh")
PLANE = ("xl", "y")
FEAT = ("xl", "y", "c")

LANES = (((1,), (1,)), ((), ()))


def dot_t(a, b, precision=HIGH):
    return lax.dot_general(a, b, LANES, precision=precision, preferred_element_type=F32)


def iota(shape, dim):
    return lax.broadcasted_iota(jnp.int32, shape, dim)


def to_row(col, offset=0):
    n = col.shape[0]
    place = iota((n, 128), 1) == iota((n, 128), 0) + offset
    return jnp.sum(jnp.where(place, col, 0.0), axis=0, keepdims=True)


def to_col(row, n, offset=0):
    place = iota((n, 128), 1) == iota((n, 128), 0) + offset
    return jnp.sum(jnp.where(place, row, 0.0), axis=1, keepdims=True)


def call(kernel, outs, *args, smem=0, hbm=0, space=pltpu.VMEM, scratch=()):
    vmem = len(args) - smem - hbm
    spaces = [pltpu.SMEM] * smem + [pltpu.VMEM] * vmem + [pl.ANY] * hbm
    args = list(args)
    for i in range(smem, smem + vmem):
        args[i] = pltpu.with_memory_space_constraint(args[i], pltpu.VMEM)
    for i in range(smem + vmem, len(args)):
        args[i] = pltpu.with_memory_space_constraint(args[i], pltpu.HBM)
    many = isinstance(outs, list)
    out_spec = pl.BlockSpec(memory_space=pltpu.VMEM)
    return pl.pallas_call(
        kernel,
        out_shape=[space(s, d) for s, d in outs] if many else space(*outs),
        in_specs=[pl.BlockSpec(memory_space=m) for m in spaces],
        out_specs=[out_spec] * len(outs) if many else out_spec,
        scratch_shapes=scratch,
        compiler_params=pltpu.CompilerParams(vmem_limit_bytes=12 << 20),
    )(*args)


def pick_kernel(own_ref, other_ref, ft_hbm, out_ref, ft_ref, sem):
    copy = pltpu.make_async_copy(ft_hbm, ft_ref, sem)
    copy.start()
    lane = iota((OWN, ROWS), 1)
    pair = iota((OWN, N_FEAT), 1) >> 1

    def masks(index_ref):
        index = index_ref[...]
        parts = []
        for p in range(N_PLANE):
            col = jnp.max(jnp.where(pair == p, index, -1), axis=1, keepdims=True)
            parts.append((lane == col).astype(F32).astype(BF16))
        return jnp.concatenate(parts, axis=0)

    own, other = masks(own_ref), masks(other_ref)
    copy.wait()
    ft = ft_ref[...]
    zero = jnp.zeros_like(ft)
    both = lax.dot_general(own, jnp.concatenate([ft, zero], axis=0), LANES, preferred_element_type=F32)
    both += lax.dot_general(other, jnp.concatenate([zero, ft], axis=0), LANES, preferred_element_type=F32)
    out_ref[...] = both.astype(BF16).reshape(N_PLANE, OWN, 2 * SLICE)


def spread_kernel(in_ref, out_ref, mine_ref):
    side, y = lax.axis_index("xl"), lax.axis_index("y")
    group = 2 * side + (y >> 2)
    mine_ref[...] = (iota((4, 128), 1) == iota((4, 128), 0) + group * 4).astype(F32)
    low = iota((OWN, 128), 1) < SLICE
    for t, offset in enumerate(OFFSETS):
        row = lax.rem(y + (offset + N_Y), N_Y)
        a = in_ref[side * N_Y + row].astype(F32)
        b = in_ref[(1 - side) * N_Y + row].astype(F32)
        own = jnp.where(low, a, pltpu.roll(b, SLICE, 1)).astype(BF16)
        other = jnp.where(low, pltpu.roll(a, SLICE, 1), b).astype(BF16)
        cols = slice(128 * t, 128 * t + 128)
        for i in range(N_EX):
            out_ref[i, 0:OWN, cols] = own
            out_ref[i, OWN : 2 * OWN, cols] = other


def diagonal():
    return iota((BLOCK, BLOCK), 0) == iota((BLOCK, BLOCK), 1)


def load_features(chunk_hbm, last_ref, ft_ref, sems):
    copies = []
    for i, chunk in enumerate(chunk_hbm):
        copies.append(pltpu.make_async_copy(chunk, ft_ref.at[128 * i : 128 * i + 128], sems.at[i]))
        copies[-1].start()
    ft_ref[128 * len(chunk_hbm) :] = last_ref[...]
    return copies


def centre_squares(cen_ref, first):
    block = cen_ref[:, first : first + OWN, :].reshape(BLOCK, WIDTH)
    squares = jnp.sum(jnp.square(block.astype(F32)), axis=1, keepdims=True)
    return jnp.sum(jnp.where(diagonal(), squares, 0.0), axis=0, keepdims=True)


def centre_dots(cen_ref, first, ft_ref):
    block = cen_ref[:, first : first + OWN, :].reshape(BLOCK, WIDTH)
    return jnp.dot(block, ft_ref[...], preferred_element_type=F32)


def other_kernel(last_ref, cen_ref, *refs):
    *chunk_hbm, out_ref, ft_ref, sems = refs
    copies = load_features(chunk_hbm, last_ref, ft_ref, sems)
    out_ref[BLOCK : BLOCK + 8, :] = jnp.zeros((8, ROWS), F32)
    out_ref[BLOCK + 1 : BLOCK + 2, 0:BLOCK] = centre_squares(cen_ref, OWN)

    def squares(start):
        return jnp.sum(jnp.square(ft_ref[start : start + 128].astype(F32)), axis=0, keepdims=True)

    row_sq = squares(128 * len(chunk_hbm))
    for i, copy in enumerate(copies):
        copy.wait()
        row_sq += squares(128 * i)
    out_ref[BLOCK : BLOCK + 1, :] = row_sq
    out_ref[0:BLOCK, :] = centre_dots(cen_ref, OWN, ft_ref)


def own_kernel(last_ref, cen_ref, *refs):
    *chunk_hbm, dots_ref, squares_ref, ft_ref, sems = refs
    copies = load_features(chunk_hbm, last_ref, ft_ref, sems)
    squares_ref[...] = jnp.broadcast_to(centre_squares(cen_ref, 0), (8, BLOCK))
    for copy in copies:
        copy.wait()
    dots_ref[...] = centre_dots(cen_ref, 0, ft_ref)


def split2(x):
    high = x.astype(BF16)
    return high, (x - high.astype(F32)).astype(BF16)


def split3(x):
    high = x.astype(BF16).astype(F32)
    rest = x - high
    mid = rest.astype(BF16).astype(F32)
    return jnp.concatenate([high, mid, rest - mid], axis=0).astype(BF16)


def fold3(y):
    n = y.shape[0] // 3
    return y[0:n] + (y[n : 2 * n] + y[2 * n : 3 * n])


def panel_kernel(
    dots_ref, squares_ref, sent_ref, labels_ref, loc_ref, recv_hbm, high_ref, low_ref, place_ref, out_ref, recv_ref, sems
):
    step = BLOCK // 4
    spans = [slice(BLOCK, BLOCK + 8)] + [slice(step * t, step * t + step) for t in range(4)]
    copies = [pltpu.make_async_copy(recv_hbm.at[r], recv_ref.at[r], sems.at[i]) for i, r in enumerate(spans)]
    for copy in copies:
        copy.start()
    place_ref[...] = (iota((BLOCK, ROWS), 1) == loc_ref[...]).astype(F32).astype(BF16)
    hit = iota((CLASSES, ROWS), 0) == labels_ref[...]
    targets = jnp.where(hit, CLASSES - 1.0, -1.0).astype(BF16)
    copies[0].wait()
    row_sq = sent_ref[BLOCK : BLOCK + 1, :] + recv_ref[BLOCK : BLOCK + 1, :]
    centre_sq = squares_ref[0:1, :] + recv_ref[BLOCK + 1 : BLOCK + 2, 0:BLOCK]
    centre_sq = jnp.sum(jnp.where(diagonal(), centre_sq, 0.0), axis=1, keepdims=True)
    row_scale = lax.rsqrt(row_sq / F + EPS)
    centre_scale = lax.rsqrt(centre_sq / F + EPS)
    for copy, r in zip(copies[1:], spans[1:]):
        copy.wait()
        dots = dots_ref[r] + recv_ref[r]
        cosine = jnp.clip(dots * row_scale * centre_scale[r], -1.0, 1.0)
        high, low = split2(jnp.exp(GAMMA * (cosine - 1.0)))
        high_ref[r] = high
        low_ref[r] = low
    rhs = (dot_t(targets, high_ref[...], None) + dot_t(targets, low_ref[...], None)) / EXAMPLES
    for i in range(N_EX):
        out_ref[i] = rhs


def times(parts, matrix_ref):
    return fold3(jnp.dot(parts, matrix_ref[...], preferred_element_type=F32))


def apply_both(vec, high_ref, low_ref, place_ref):
    parts = split3(vec)
    k = times(parts, high_ref) + times(parts, low_ref)
    return k, k / EXAMPLES + LAMBDA * times(parts, place_ref)


def apply_normal(k, high_ref, low_ref, place_ref):
    parts = split3(k)

    def times(matrix):
        return fold3(dot_t(parts, matrix, None))

    return (times(high_ref[...]) + times(low_ref[...])) / EXAMPLES + LAMBDA * times(place_ref[...])


def total(ref):
    acc = ref[0]
    for i in range(1, ref.shape[0]):
        acc = acc + ref[i]
    return acc


def put_chunks(out_ref, vec, stride, slot):
    for s in range(N_FEAT):
        g, l = s // 8, s % 8
        out_ref[s * stride + slot] = vec[4 * g : 4 * g + 4, 128 * l : 128 * l + 128]


def take_chunks(in_ref, stride, out_ref):
    for s in range(N_FEAT):
        g, l = s // 8, s % 8
        out_ref[4 * g : 4 * g + 4, 128 * l : 128 * l + 128] = in_ref[s * stride]


def sum_slot(ref, stride, slot):
    acc = ref[slot]
    for s in range(1, N_FEAT):
        acc = acc + ref[s * stride + slot]
    return acc


def first_kernel(recv_ref, pre_ref, high_ref, low_ref, place_ref, rhs_ref, u_ref, out_ref):
    rhs = total(recv_ref)
    u = dot_t(rhs, pre_ref[...])
    rhs_ref[...] = rhs
    u_ref[...] = u
    k, g = apply_both(u, high_ref, low_ref, place_ref)
    put_chunks(out_ref, k, 2, 0)
    put_chunks(out_ref, g, 2, 1)


def chunk_kernel(recv_ref, chunk_ref, out_ref):
    k = sum_slot(recv_ref, 2, 0)
    chunk_ref[0] = k
    chunk_ref[1] = sum_slot(recv_ref, 2, 1)
    for s in range(N_FEAT):
        out_ref[s] = k


def normal_kernel(recv_ref, high_ref, low_ref, place_ref, k_ref, out_ref):
    take_chunks(recv_ref, 1, k_ref)
    image = apply_normal(k_ref[...], high_ref, low_ref, place_ref)
    for i in range(N_EX):
        out_ref[i] = image


def second_kernel(recv_ref, pre_ref, high_ref, low_ref, place_ref, rhs_ref, u_ref, image_ref, v_ref, out_ref):
    image = total(recv_ref)
    v = dot_t(image, pre_ref[...])
    image_ref[...] = image
    v_ref[...] = v
    k, g = apply_both(v, high_ref, low_ref, place_ref)
    put_chunks(out_ref, k, 3, 0)
    put_chunks(out_ref, g, 3, 1)
    u = u_ref[...]
    row = to_row(jnp.sum(rhs_ref[...] * u, axis=1, keepdims=True), 0)
    row = row + to_row(jnp.sum(u * image, axis=1, keepdims=True), CLASSES)
    row = row + to_row(jnp.sum(v * image, axis=1, keepdims=True), 2 * CLASSES)
    row = jnp.broadcast_to(row, (4, 128))
    for s in range(N_FEAT):
        out_ref[s * 3 + 2] = row


def scalars(row):
    rz = to_col(row, CLASSES, 0)
    uu = to_col(row, CLASSES, CLASSES)
    vu = to_col(row, CLASSES, 2 * CLASSES)
    alpha = rz / uu
    return rz, uu, vu, alpha, alpha * (vu / uu) - 1.0


def step_kernel(mine_ref, recv_ref, chunk_ref, rhs_ref, u_ref, image_ref, v_ref, scal_ref, out_ref):
    row = sum_slot(recv_ref, 3, 2)[0:1]
    scal_ref[...] = jnp.broadcast_to(row, (8, 128))
    _, _, _, alpha, guess = scalars(row)
    residual = rhs_ref[...] - alpha * image_ref[...]
    z = u_ref[...] - alpha * v_ref[...]
    rz = to_row(jnp.sum(residual * z, axis=1, keepdims=True))
    mine = mine_ref[...]
    alpha_mine = jnp.sum(mine * to_row(alpha), axis=1, keepdims=True)
    guess_mine = jnp.sum(mine * to_row(guess), axis=1, keepdims=True)
    k, g = chunk_ref[0], chunk_ref[1]
    kd = (k - alpha_mine * sum_slot(recv_ref, 3, 0)) + guess_mine * k
    gd = (g - alpha_mine * sum_slot(recv_ref, 3, 1)) + guess_mine * g
    quad = jnp.sum(kd * gd, axis=1, keepdims=True)
    quad_row = jnp.sum(mine * quad, axis=0, keepdims=True)
    which = iota((4, 128), 0)
    tail = jnp.where(which == 0, rz, jnp.where(which == 1, quad_row, 0.0))
    for s in range(N_FEAT):
        out_ref[s * 2] = kd
        out_ref[s * 2 + 1] = tail


def gather_kernel(recv_ref, kd_ref, tail_ref, out_ref):
    take_chunks(recv_ref, 2, kd_ref)
    tail = sum_slot(recv_ref, 2, 1)
    tail_ref[...] = tail
    for i in range(N_EX):
        out_ref[i] = tail[1:2]


def last_kernel(recv_ref, tail_ref, scal_ref, k_ref, kd_ref, out_ref):
    quad = to_col(total(recv_ref), CLASSES)
    rz_next = to_col(tail_ref[0:1, :], CLASSES)
    rz, uu, vu, alpha, guess = scalars(scal_ref[0:1, :])
    delta = rz_next / rz - guess
    slope = (uu - alpha * vu) + guess * uu
    alpha_next = rz_next / (quad + delta * (2.0 * slope + delta * uu))
    k = k_ref[...]
    out_ref[...] = alpha * k + alpha_next * (kd_ref[...] + delta * k)


def predict(features, centre_index, labels, precond):
    ex_index = lax.axis_index(EX)
    feat_index = lax.axis_index(FEAT)
    core = lax.axis_index("c")
    local = centre_index[:, 0, :] - ex_index * ROWS
    ft_local = features.T
    swapped = lax.ppermute(ft_local, "xl", [(0, 1), (1, 0)])
    here = jnp.concatenate([ft_local, swapped], axis=0)
    up = [(i, (i + 1) % N_Y) for i in range(N_Y)]
    down = [(i, (i - 1) % N_Y) for i in range(N_Y)]
    chunks = [here]
    below = above = here
    for _ in range(3):
        below = lax.ppermute(below, "y", up)
        above = lax.ppermute(above, "y", down)
        chunks += [below, above]
    chunks.append(lax.ppermute(below, "y", up))

    index = centre_index[:, 0, :].T - ex_index * ROWS
    ours = (iota((OWN, N_FEAT), 1) & 1) == core
    picked = call(
        pick_kernel, ((N_PLANE, OWN, 2 * SLICE), BF16), jnp.where(ours, index, -1), jnp.where(ours, -1, index), ft_local,
        hbm=1, scratch=[pltpu.VMEM((SLICE, ROWS), BF16), pltpu.SemaphoreType.DMA],
    )
    picked = lax.all_to_all(picked, PLANE, 0, 0, tiled=True)
    spread, mine = call(spread_kernel, [((N_EX, 2 * OWN, WIDTH), BF16), ((4, 128), F32)], picked)
    cen = lax.all_to_all(spread, EX, 0, 0, tiled=True)

    own_rows = lax.dynamic_index_in_dim(local, feat_index, 0, keepdims=False)
    slot = lax.iota(jnp.int32, N_EX)[:, None] == ex_index
    loc = jnp.where(slot, own_rows[None, :], -1).reshape(BLOCK, 1)

    dots_t = ((BLOCK, ROWS), F32)
    operands = (chunks[-1], cen, *chunks[:-1])
    still = len(chunks) - 1
    scratch = [pltpu.VMEM((WIDTH, ROWS), BF16), pltpu.SemaphoreType.DMA((still,))]
    sent = call(other_kernel, ((BLOCK + 8, ROWS), F32), *operands, hbm=still, scratch=scratch)
    got = lax.ppermute(sent, "c", [(0, 1), (1, 0)])
    own, own_sq = call(own_kernel, [dots_t, ((8, BLOCK), F32)], *operands, hbm=still, scratch=scratch)
    half_t = ((BLOCK, ROWS), BF16)
    high, low, place, part = call(
        panel_kernel, [half_t, half_t, half_t, ((N_EX, CLASSES, BLOCK), F32)],
        own, own_sq, sent, labels.reshape(1, ROWS), loc, got, hbm=1,
        scratch=[pltpu.VMEM(sent.shape, F32), pltpu.SemaphoreType.DMA((5,))],
    )
    vec = ((CLASSES, BLOCK), F32)
    part = lax.all_to_all(part, EX, 0, 0, tiled=True)
    rhs, u, part = call(first_kernel, [vec, vec, ((N_FEAT * 2, 4, 128), F32)], part, precond, high, low, place)
    part = lax.all_to_all(part, FEAT, 0, 0, tiled=True)
    chunk, part = call(chunk_kernel, [((2, 4, 128), F32), ((N_FEAT, 4, 128), F32)], part)
    part = lax.all_to_all(part, FEAT, 0, 0, tiled=True)
    k, part = call(normal_kernel, [((CLASSES, ROWS), F32), ((N_EX, CLASSES, BLOCK), F32)], part, high, low, place)
    part = lax.all_to_all(part, EX, 0, 0, tiled=True)
    image, v, part = call(
        second_kernel, [vec, vec, ((N_FEAT * 3, 4, 128), F32)],
        part, precond, high, low, place, rhs, u,
    )
    part = lax.all_to_all(part, FEAT, 0, 0, tiled=True)
    scal, part = call(
        step_kernel, [((8, 128), F32), ((N_FEAT * 2, 4, 128), F32)],
        mine, part, chunk, rhs, u, image, v,
    )
    part = lax.all_to_all(part, FEAT, 0, 0, tiled=True)
    kd, tail, part = call(gather_kernel, [((CLASSES, ROWS), F32), ((4, 128), F32), ((N_EX, 1, 128), F32)], part)
    part = lax.all_to_all(part, EX, 0, 0, tiled=True)
    out = call(last_kernel, ((CLASSES, ROWS), F32), part, tail, scal, k, kd, space=jax.ShapeDtypeStruct)
    return out.T


def solution(mesh):
    fine = Mesh(mesh.devices.reshape(8, 2, 2, 8, 2), ("z", "xh", "xl", "y", "c"))
    in_specs = (P(EX, FEAT), P(None, EX, None), P(EX), P(FEAT, None))
    return jax.shard_map(predict, mesh=fine, in_specs=in_specs, out_specs=P(EX, None), check_vma=False)
```
